32 devices in a mesh: groups: 2 (over y), cable: 4 (over z), bins: 2 (over x), pairs: 2 (over core).
Axes of the slice: x: 2, y: 2, z: 4, core: 2. Of those that a mesh axis runs over, the one named last changes fastest.
Arguments:
- spectra: bfloat16 [4, 16, 256, 2048], P('groups', None, 'cable', 'bins'), parts along dimension 0, may hold values from -6 to 6
- counts: int32 [8], P(('groups', 'cable')), parts along dimension 0, may hold values from 1 to 4, as said below
- owners: int32 [8, 4], P(('groups', 'cable')), parts along dimension 0, may hold values from 0 to 1
Outputs:
- stacks: float32 [4, 4, 320, 2048], P('groups', 'cable', 'pairs', 'bins'), parts along dimension 0
The draws below stay inside these ranges and needn't reach their ends.
There are 2 independent parts, one for each index of `groups`. The reference program is written for one: setup_inputs(seed, part) draws one part's arguments, and reference() takes and returns one part's arrays. A program takes and returns all parts, laid end to end along the dimension named above; each array names one. Nothing has to cross between parts.
Inputs may be any that keep to these rules, and one draw needn't show every extreme that they name: `counts`: block 0 keeps 4 offsets and block 1 keeps 1.
All inputs are finite; a program needn't handle non-finite values.
Results may differ from the reference program's by a relative error of at most 0.0017.
Values may be sent and summed in bfloat16 or wider, within the bound.
A program may use at most 128 MiB of HBM per device.

```python
import math
import jax
import jax.numpy as jnp
from jax import lax

NF = 2048
BLOCK_CH = 64
WINDOWS = 16
REACH = 3
HALF_WIDTH = 32
BLOCKS = 4
CH = 256
LAGS = 320


def draw_counts(key, part):
    values = jax.random.randint(key, (BLOCKS,), 1, REACH + 2)
    return values.at[0].set(REACH + 1).at[1].set(1)


def touch_ends(drawn, key, low, top_value):
    longest = drawn.shape.index(max(drawn.shape))
    spots = []
    for shift in (0, 1):
        where = [jax.random.randint(jax.random.fold_in(key, axis), (), 0, length) for axis, length in enumerate(drawn.shape)]
        where[longest] = (where[longest] + shift) % drawn.shape[longest]
        spots.append(tuple(where))
    return drawn.at[spots[0]].set(low).at[spots[1]].set(top_value)


def steps_of(key, extent, split, low, largest):
    gain = 1.0
    for dim, shards_of in split:
        draws = jax.random.uniform(jax.random.fold_in(jax.random.fold_in(key, 6), dim), (shards_of,), jnp.float32, low / len(split), largest / len(split))
        gain = gain * jnp.repeat(jnp.exp(draws), extent[dim] // shards_of).reshape((-1,) + (1,) * (len(extent) - 1 - dim))
    return gain


def gaussian(stream_key, shape, spread, reach, split=(), kind=jnp.bfloat16):
    level = steps_of(stream_key, shape, split, -0.22, 0.18) if split else 1.0
    array = jax.random.normal(stream_key, shape, jnp.float32) * spread * level
    return jnp.minimum(jnp.maximum(array, -reach), reach).astype(kind)


def setup_inputs(seed: int = 0, part: int = 0) -> dict:
    arg_keys = jax.random.split(jax.random.key(seed), 4)
    part_splits = jax.random.split(jax.random.fold_in(arg_keys[3], part), 4)
    spectra = gaussian(part_splits[0], (2, WINDOWS, CH, NF), 1.0, 6.0, ((2, 4), (3, 2)))
    counts = draw_counts(jax.random.fold_in(jax.random.fold_in(arg_keys[3], part), 71), part)
    owners = touch_ends(jax.random.randint(part_splits[2], (BLOCKS, REACH + 1), 0, 2), jax.random.fold_in(part_splits[2], 1), 0, 1).astype(jnp.int32)
    return dict(spectra=spectra, counts=counts, owners=owners)


epsilon = 1e-06

def whiten_rows(spectra):
    real_part = spectra[0].astype(jnp.float32)
    imag_part = spectra[1].astype(jnp.float32)
    power_sum = real_part * real_part + imag_part * imag_part
    padded = jnp.pad(power_sum, ((0, 0), (0, 0), (HALF_WIDTH, HALF_WIDTH)))
    window_len = 2 * HALF_WIDTH + 1
    window_sum = lax.reduce_window(padded, jnp.zeros((), padded.dtype), lax.add, (1, 1, window_len), (1, 1, 1), 'VALID')
    inverse_amp = lax.rsqrt(window_sum / window_len + epsilon)
    return jnp.stack([(real_part * inverse_amp).astype(jnp.bfloat16), (imag_part * inverse_amp).astype(jnp.bfloat16)])

def cross_blocks(source, receiver):
    left_real = jnp.concatenate([source[0], source[1]], axis=0).astype(jnp.float32)
    left_imag = jnp.concatenate([source[1], -source[0]], axis=0).astype(jnp.float32)
    right_both = jnp.concatenate([receiver[0], receiver[1]], axis=0).astype(jnp.float32)
    factor = 1.0 / math.sqrt(source.shape[1] * source.shape[2])
    corr_real = (jnp.einsum('wif,wjf->fij', left_real, right_both) * factor).astype(jnp.bfloat16)
    corr_imag = (jnp.einsum('wif,wjf->fij', left_imag, right_both) * factor).astype(jnp.bfloat16)
    return (corr_real, corr_imag)

def lag_stack(pair_block):
    values = pair_block.astype(jnp.float32)[:, ::-1, :]
    freq_count, row_count, col_count = values.shape
    padded = jnp.pad(values, ((0, 0), (0, 0), (0, row_count)))
    flattened = padded.reshape(freq_count, row_count * (col_count + row_count))
    flattened = flattened[:, :row_count * (col_count + row_count - 1)]
    return flattened.reshape(freq_count, row_count, col_count + row_count - 1).sum(axis=1)

def reference(spectra, counts, owners):
    white = whiten_rows(spectra)
    stacks = jnp.zeros((2, BLOCKS, LAGS, NF), jnp.float32)
    for block_index in range(BLOCKS):
        source = white[:, :, block_index * BLOCK_CH:(block_index + 1) * BLOCK_CH]
        live_count = jnp.minimum(counts[block_index], BLOCKS - block_index)
        for offset in range(REACH + 1):
            if block_index + offset < BLOCKS:
                far_index = block_index + offset
                receiver = white[:, :, far_index * BLOCK_CH:(far_index + 1) * BLOCK_CH]
                corr_real, corr_imag = cross_blocks(source, receiver)
                lag_piece = jnp.stack([lag_stack(corr_real), lag_stack(corr_imag)])
                lag_piece = jnp.swapaxes(lag_piece, 1, 2)[:, None]
                weight = (offset < live_count).astype(jnp.float32)
                target = (block_index + offset * owners[block_index, offset]).astype(jnp.int32)
                first_lag = (jnp.int32(0), target, jnp.int32(offset * BLOCK_CH), jnp.int32(0))
                current = lax.dynamic_slice(stacks, first_lag, lag_piece.shape)
                stacks = lax.dynamic_update_slice(stacks, current + weight * lag_piece, first_lag)
    return stacks
```

```python
import math

import jax
import jax.numpy as jnp
import numpy as np
from jax import lax
from jax.experimental import pallas as pl
from jax.experimental.pallas import tpu as pltpu
from jax.sharding import PartitionSpec as P

REACH = 3
HALF_WIDTH = 32


epsilon = 1e-06
band_rows = 16


def with_halo(x, sides, width):
    for axis, dim in sides:
        count, length = (lax.axis_size(axis), x.shape[dim])
        up = [(i, (i + 1) % count) for i in range(count - 1)]
        down = [(j, i) for i, j in up]
        last = lax.slice_in_dim(x, length - width, length, axis=dim)
        first = lax.slice_in_dim(x, 0, width, axis=dim)
        before = lax.ppermute(last, axis, up)
        after = lax.ppermute(first, axis, down)
        x = jnp.concatenate([before, x, after], axis=dim)
    return x


def from_behind(block, axis, distance):
    devices = range(lax.axis_size(axis))
    route = [(i - distance, i) for i in devices if i - distance in devices]
    return lax.ppermute(block, axis, route)


def whiten_rows(spectra):
    real_part = spectra[0].astype(jnp.float32)
    imag_part = spectra[1].astype(jnp.float32)
    power_sum = real_part * real_part + imag_part * imag_part
    padded = with_halo(power_sum, (("bins", 2),), HALF_WIDTH)
    window_len = 2 * HALF_WIDTH + 1
    window_sum = lax.reduce_window(
        padded, jnp.zeros((), padded.dtype), lax.add, (1, 1, window_len), (1, 1, 1), "VALID"
    )
    inverse_amp = lax.rsqrt(window_sum / window_len + epsilon)
    return jnp.stack(
        [
            (real_part * inverse_amp).astype(jnp.bfloat16),
            (imag_part * inverse_amp).astype(jnp.bfloat16),
        ]
    )


def make_lag_table(col_count):
    flattened = jnp.arange(band_rows * col_count)
    row_of = flattened // col_count
    col_of = flattened % col_count
    lag_lanes = jnp.arange(col_count + band_rows - 1)
    return (lag_lanes[None, :] == (col_of - row_of + band_rows - 1)[:, None]).astype(jnp.bfloat16)


def lag_stack(pair_block, lag_table):
    freq_count, row_count, col_count = pair_block.shape
    group_count = row_count // band_rows
    grouped = pair_block.reshape(freq_count, group_count, band_rows * col_count)
    banded = jnp.einsum("fgk,ku->fgu", grouped, lag_table, preferred_element_type=jnp.float32)
    lag_sums = jnp.zeros((freq_count, col_count + row_count - 1), jnp.float32)
    for row_group in range(group_count):
        first_lag = row_count - band_rows * (row_group + 1)
        lag_sums = lag_sums.at[:, first_lag : first_lag + col_count + band_rows - 1].add(
            banded[:, row_group]
        )
    return lag_sums.T


def correlate(left_rows, right_rows, factor, lag_table):
    left_real = jnp.concatenate([left_rows[0], left_rows[1]], axis=0)
    left_imag = jnp.concatenate([left_rows[1], -left_rows[0]], axis=0)
    right_both = jnp.concatenate([right_rows[0], right_rows[1]], axis=0)
    corr_real = (
        jnp.einsum("wif,wjf->fij", left_real, right_both, preferred_element_type=jnp.float32)
        * factor
    ).astype(jnp.bfloat16)
    corr_imag = (
        jnp.einsum("wif,wjf->fij", left_imag, right_both, preferred_element_type=jnp.float32)
        * factor
    ).astype(jnp.bfloat16)
    return jnp.stack([lag_stack(corr_real, lag_table), lag_stack(corr_imag, lag_table)])


def general_shards(spectra, counts, owners):
    pair_devs = lax.axis_size("pairs")
    member = lax.axis_index("pairs")
    channels = spectra.shape[2]
    half_rows = channels // pair_devs
    source = whiten_rows(spectra)
    receiver = lax.dynamic_slice_in_dim(source, member * half_rows, half_rows, 2)
    block_count = lax.axis_size("cable")
    cable_index = lax.axis_index("cable")
    live_count = jnp.minimum(counts[0], block_count - cable_index)
    panels = {0: receiver}
    for offset in range(1, REACH + 1):
        panels[offset] = from_behind(receiver, "cable", -offset)
    factor = 1.0 / math.sqrt(source.shape[1] * channels)
    lag_table = make_lag_table(half_rows)
    freq_count = source.shape[3]
    stacks = jnp.zeros((2, (REACH + 2) * channels, freq_count), jnp.float32)
    for offset in range(REACH + 1):
        lag_piece = correlate(source, panels[offset], factor, lag_table)
        weight = (offset < live_count).astype(jnp.float32)
        if offset == 0:
            kept_here = weight * lag_piece
        else:
            sent_away = owners[0, offset].astype(jnp.float32)
            arrived = from_behind(weight * sent_away * lag_piece, "cable", offset)
            kept_here = weight * (1.0 - sent_away) * lag_piece + arrived
        first_lag = offset * channels + member * half_rows
        current = lax.dynamic_slice_in_dim(stacks, first_lag, kept_here.shape[1], 1)
        stacks = lax.dynamic_update_slice_in_dim(stacks, current + kept_here, first_lag, 1)
    summed = lax.psum_scatter(stacks, "pairs", scatter_dimension=1, tiled=True)
    return summed[:, None]


EDGE = 128
BAND = 128
GROUP = 4
F32 = jnp.float32
MESH = pl.DeviceIdType.MESH


def channel_transforms(channels, factor):
    points = 2 * channels
    index = np.arange(points)
    angle = 2 * np.pi * np.outer(index, np.arange(channels)) / points
    cos, sin = np.cos(angle), np.sin(angle)
    full = np.block([[cos, sin], [-sin, cos]])
    high = full.astype(jnp.bfloat16)
    low = (full - high.astype(np.float64)).astype(jnp.bfloat16)
    forward = np.concatenate([high, low], axis=1)
    angle = 2 * np.pi * np.outer(index - (channels - 1), index) / points
    cos, sin = np.cos(angle), np.sin(angle)
    cos[-1], sin[-1] = 0.0, 0.0
    inverse = np.block([[cos, sin], [-sin, cos]]) * (factor / points)
    return jnp.asarray(forward), jnp.asarray(inverse.astype(np.float32))


def stack_kernel(
    x_ref, flag_ref, forward_ref, inverse_ref, out_ref,
    white, far, back, spec, other, sums, sums_back, stack, piece_out, piece_back, piece_in, arrived, swapped, seen,
    chain_send, chain_recv, back_send, back_recv, piece_send, piece_recv,
    next_send, next_recv, swap_send, swap_recv, flag_send, flag_recv,
):
    windows, channels, length = x_ref.shape[1:]
    half = length - 2 * EDGE
    bands, groups = half // BAND, windows // GROUP
    points = 2 * channels
    kept = out_ref.shape[1]
    blocks, halves = lax.axis_size("cable"), lax.axis_size("pairs")
    z, m = lax.axis_index("cable"), lax.axis_index("pairs")
    onward = {"cable": lax.rem(z + 1, blocks)}
    backward = {"cable": lax.rem(z + blocks - 1, blocks)}
    partner = {"pairs": lax.rem(m + 1, halves)}

    def remote(source, target, send, recv, device):
        return pltpu.make_async_remote_copy(
            src_ref=source, dst_ref=target, send_sem=send, recv_sem=recv, device_id=device, device_id_type=MESH
        )

    def first_hop(s):
        return remote(white.at[s], far.at[s], chain_send.at[s], chain_recv.at[s], onward)

    def next_hop(s):
        return remote(far.at[s], far.at[s], chain_send.at[s], chain_recv.at[s], onward)

    def back_hop(s):
        return remote(white.at[s], back.at[s], back_send.at[s], back_recv.at[s], backward)

    def to_first(c, slot):
        return remote(piece_out.at[c], piece_in.at[slot, c], piece_send.at[c], piece_recv.at[slot, c], {"cable": 0})

    def to_next(c):
        return remote(piece_back.at[c], arrived.at[c], next_send.at[c], next_recv.at[c], onward)

    def swap(c):
        rows = pl.ds(pl.multiple_of((1 - m) * kept, 8), kept)
        return remote(stack.at[c, :, rows], swapped.at[c], swap_send.at[c], swap_recv.at[c], partner)

    def flags_to(block):
        return remote(flag_ref, seen, flag_send.at[block - 1], flag_recv.at[0], {"cable": block})

    barrier = pltpu.get_barrier_semaphore()
    for step in range(1, blocks):
        pl.semaphore_signal(barrier, inc=1, device_id={"cable": lax.rem(z + step, blocks)}, device_id_type=MESH)
    pl.semaphore_signal(barrier, inc=1, device_id=partner, device_id_type=MESH)
    pl.semaphore_wait(barrier, blocks)

    @pl.when(z == 0)
    def _():
        for block in range(1, blocks):
            flags_to(block).start()

    def whiten(q, carry):
        for i in range(GROUP):
            real = x_ref[0, q * GROUP + i].astype(F32)
            imag = x_ref[1, q * GROUP + i].astype(F32)
            power = real * real + imag * imag
            total, width = power, 1
            while width < 2 * HALF_WIDTH:
                total = total + pltpu.roll(total, width, 1)
                width *= 2
            total = total + pltpu.roll(power, width, 1)
            total = pltpu.roll(total, length - HALF_WIDTH, 1)[:, EDGE : EDGE + half]
            gain = lax.rsqrt(total / (2 * HALF_WIDTH + 1) + epsilon)
            real = (real[:, EDGE : EDGE + half] * gain).astype(jnp.bfloat16)
            imag = (imag[:, EDGE : EDGE + half] * gain).astype(jnp.bfloat16)
            for c in range(bands):
                white[c * groups + q, i, :channels] = real[:, c * BAND : (c + 1) * BAND]
                white[c * groups + q, i, channels:] = imag[:, c * BAND : (c + 1) * BAND]

        @pl.when(z == 0)
        def _():
            first_hop(q).start()

        @pl.when(z == blocks - 1)
        def _():
            back_hop(q).start()

        return carry

    lax.fori_loop(0, groups, whiten, 0)

    @pl.when(z == 0)
    def _():
        @pl.loop(groups, bands * groups)
        def _(s):
            first_hop(s).start()

    @pl.when(z == blocks - 1)
    def _():
        @pl.loop(groups, bands * groups)
        def _(s):
            back_hop(s).start()

    def transform(buffer, s):
        wide = jnp.concatenate([buffer[s, i] for i in range(GROUP)], axis=1)
        return jnp.dot(forward_ref[...], jnp.concatenate([wide, wide], axis=0), preferred_element_type=F32)

    tile = 32

    def power_into(total, s):
        for k in range(0, points, tile):
            gained = total[k : k + tile]
            for i in range(GROUP):
                lanes = slice(i * BAND, (i + 1) * BAND)
                real = spec[s, k : k + tile, lanes]
                imag = spec[s, points + k : points + k + tile, lanes]
                gained = gained + (real * real + imag * imag)
            total[k : k + tile] = gained

    def cross_into(total, s, sign):
        for k in range(0, points, tile):
            gained_real = total[k : k + tile]
            gained_imag = total[points + k : points + k + tile]
            for i in range(GROUP):
                lanes = slice(i * BAND, (i + 1) * BAND)
                own_real = spec[s, k : k + tile, lanes]
                own_imag = spec[s, points + k : points + k + tile, lanes]
                real = other[k : k + tile, lanes]
                imag = other[points + k : points + k + tile, lanes]
                gained_real = gained_real + (own_real * real + own_imag * imag)
                if sign > 0:
                    gained_imag = gained_imag + (own_imag * real - own_real * imag)
                else:
                    gained_imag = gained_imag + (own_real * imag - own_imag * real)
            total[k : k + tile] = gained_real
            total[points + k : points + k + tile] = gained_imag

    def lags_of(values, columns):
        return jnp.dot(
            inverse_ref[:, :columns], values, preferred_element_type=F32, precision=lax.Precision.HIGHEST
        )

    def add_piece(c, first, piece):
        rows = pl.ds(first, points)
        stack[c, 0, rows] += piece[:points]
        stack[c, 1, rows] += piece[points:]

    def own_band(c, carry):
        sums[...] = jnp.zeros_like(sums)

        def step(q, inner):
            s = c * groups + q
            spec[s] = transform(white, s)
            power_into(sums, s)
            return inner

        lax.fori_loop(0, groups, step, 0)
        stack[c] = jnp.zeros(stack.shape[1:], F32)
        add_piece(c, 0, flag_ref[REACH + 1 : REACH + 2, :] * lags_of(sums[:points], points))
        return carry

    lax.fori_loop(0, bands, own_band, 0)

    @pl.when(z > 0)
    def _():
        flags_to(1).wait_recv()

        def far_band(c, carry):
            sums[...] = jnp.zeros_like(sums)
            sums_back[...] = jnp.zeros_like(sums_back)

            def step(q, inner):
                s = c * groups + q
                next_hop(s).wait_recv()

                @pl.when(z < blocks - 1)
                def _():
                    next_hop(s).start()

                other[...] = transform(far, s)
                cross_into(sums, s, -1)

                @pl.when(z == blocks - 2)
                def _():
                    back_hop(s).wait_recv()
                    other[...] = transform(back, s)
                    cross_into(sums_back, s, 1)

                return inner

            lax.fori_loop(0, groups, step, 0)
            piece = lags_of(sums[...], 2 * points)
            piece_out[c] = piece
            to_first(c, z - 1).start()
            counted = seen[pl.ds(z, 1), :] * seen[pl.ds(REACH + 1 + z, 1), :]
            add_piece(c, pl.multiple_of(z * channels, 8), counted * piece)

            @pl.when(z == blocks - 2)
            def _():
                piece = flag_ref[REACH + 2 : REACH + 3, :] * lags_of(sums_back[...], 2 * points)
                sent = flag_ref[1:2, :]
                piece_back[c] = sent * piece
                to_next(c).start()
                add_piece(c, channels, (1.0 - sent) * piece)

            @pl.when(z == blocks - 1)
            def _():
                to_next(c).wait_recv()
                add_piece(c, channels, arrived[c])

            swap(c).start()
            return carry

        lax.fori_loop(0, bands, far_band, 0)

    @pl.when(z == 0)
    def _():
        def near_band(c, carry):
            for offset in range(1, blocks):
                to_first(c, offset - 1).wait_recv()
                counted = (1.0 - flag_ref[offset : offset + 1, :]) * flag_ref[REACH + 1 + offset : REACH + 2 + offset, :]
                add_piece(c, offset * channels, counted * piece_in[offset - 1, c])
            swap(c).start()
            return carry

        lax.fori_loop(0, bands, near_band, 0)

    def collect(c, carry):
        mine = pl.ds(pl.multiple_of(m * half + c * BAND, BAND), BAND)
        theirs = pl.ds(pl.multiple_of((1 - m) * half + c * BAND, BAND), BAND)
        out_ref[:, :, mine] = stack[c, :, pl.ds(pl.multiple_of(m * kept, 8), kept)]
        swap(c).wait_recv()
        out_ref[:, :, theirs] = swapped[c]
        swap(c).wait_send()
        return carry

    lax.fori_loop(0, bands, collect, 0)

    @pl.when(z < blocks - 1)
    def _():
        @pl.loop(0, bands * groups)
        def _(s):
            next_hop(s).wait_send()

    @pl.when(z == blocks - 1)
    def _():
        @pl.loop(0, bands * groups)
        def _(s):
            back_hop(s).wait_send()

    @pl.when(z > 0)
    def _():
        @pl.loop(0, bands)
        def _(c):
            to_first(c, z - 1).wait_send()

    @pl.when(z == blocks - 2)
    def _():
        @pl.loop(0, bands)
        def _(c):
            to_next(c).wait_send()

    @pl.when(z == 0)
    def _():
        for block in range(1, blocks):
            flags_to(block).wait_send()


def four_block_shards(spectra, counts, owners):
    parts, windows, channels, bins = spectra.shape
    halves, member = lax.axis_size("pairs"), lax.axis_index("pairs")
    blocks, z = lax.axis_size("cable"), lax.axis_index("cable")
    half, points = bins // halves, 2 * channels
    pad = jnp.zeros((parts, windows, channels, EDGE - HALF_WIDTH), spectra.dtype)
    padded = with_halo(spectra, (("bins", 3),), HALF_WIDTH)
    padded = jnp.concatenate([pad, padded, pad], axis=3)
    padded = lax.dynamic_slice_in_dim(padded, member * half, half + 2 * EDGE, 3)
    live = jnp.minimum(counts[0], blocks - z)
    weights = (jnp.arange(REACH + 1) < live).astype(F32)
    flags = jnp.concatenate([owners[0].astype(F32), weights])
    flags = jnp.broadcast_to(flags[:, None], (2 * (REACH + 1), BAND))
    forward, inverse = channel_transforms(channels, 1.0 / math.sqrt(windows * channels))
    bands, groups = half // BAND, windows // GROUP
    pieces = bands * groups
    rows = (REACH + 2) * channels
    kept = rows // halves
    block = pltpu.VMEM((pieces, GROUP, points, BAND), jnp.bfloat16)
    lags = pltpu.VMEM((bands, 2 * points, BAND), F32)
    dma = pltpu.SemaphoreType.DMA
    out = pl.pallas_call(
        stack_kernel,
        out_shape=jax.ShapeDtypeStruct((2, kept, bins), F32),
        in_specs=[pl.BlockSpec(memory_space=pltpu.VMEM)] * 4,
        out_specs=pl.BlockSpec(memory_space=pltpu.VMEM),
        scratch_shapes=[
            block, block, block,
            pltpu.VMEM((pieces, 2 * points, GROUP * BAND), F32),
            pltpu.VMEM((2 * points, GROUP * BAND), F32),
            pltpu.VMEM((2 * points, BAND), F32),
            pltpu.VMEM((2 * points, BAND), F32),
            pltpu.VMEM((bands, 2, rows, BAND), F32),
            lags, lags,
            pltpu.VMEM((blocks - 1, bands, 2 * points, BAND), F32),
            lags,
            pltpu.VMEM((bands, 2, kept, BAND), F32),
            pltpu.VMEM(flags.shape, F32),
            dma((pieces,)), dma((pieces,)), dma((pieces,)), dma((pieces,)),
            dma((bands,)), dma((blocks - 1, bands)),
            dma((bands,)), dma((bands,)), dma((bands,)), dma((bands,)),
            dma((blocks - 1,)), dma((1,)),
        ],
        compiler_params=pltpu.CompilerParams(
            collective_id=0, has_side_effects=True, vmem_limit_bytes=60 * 1024 * 1024
        ),
    )(padded, flags, forward, inverse)
    return out[:, None]


def solution(mesh):
    sizes = dict(mesh.shape)
    fits = sizes["cable"] == REACH + 1 and sizes["pairs"] == 2
    shards = four_block_shards if fits else general_shards
    placed = (
        P("groups", None, "cable", "bins"),
        P(("groups", "cable")),
        P(("groups", "cable"), None),
    )
    return jax.shard_map(
        shards,
        mesh=mesh,
        in_specs=placed,
        out_specs=P("groups", "cable", "pairs", "bins"),
        check_vma=False,
    )
```

```python
import math

import jax
import jax.numpy as jnp
import numpy as np
from jax import lax
from jax.experimental import pallas as pl
from jax.experimental.pallas import tpu as pltpu
from jax.sharding import PartitionSpec as P

REACH = 3
HALF_WIDTH = 32


epsilon = 1e-06
band_rows = 16


def with_halo(x, sides, width):
    for axis, dim in sides:
        count, length = (lax.axis_size(axis), x.shape[dim])
        up = [(i, (i + 1) % count) for i in range(count - 1)]
        down = [(j, i) for i, j in up]
        last = lax.slice_in_dim(x, length - width, length, axis=dim)
        first = lax.slice_in_dim(x, 0, width, axis=dim)
        before = lax.ppermute(last, axis, up)
        after = lax.ppermute(first, axis, down)
        x = jnp.concatenate([before, x, after], axis=dim)
    return x


def from_behind(block, axis, distance):
    devices = range(lax.axis_size(axis))
    route = [(i - distance, i) for i in devices if i - distance in devices]
    return lax.ppermute(block, axis, route)


def whiten_rows(spectra):
    real_part = spectra[0].astype(jnp.float32)
    imag_part = spectra[1].astype(jnp.float32)
    power_sum = real_part * real_part + imag_part * imag_part
    padded = with_halo(power_sum, (("bins", 2),), HALF_WIDTH)
    window_len = 2 * HALF_WIDTH + 1
    window_sum = lax.reduce_window(
        padded, jnp.zeros((), padded.dtype), lax.add, (1, 1, window_len), (1, 1, 1), "VALID"
    )
    inverse_amp = lax.rsqrt(window_sum / window_len + epsilon)
    return jnp.stack(
        [
            (real_part * inverse_amp).astype(jnp.bfloat16),
            (imag_part * inverse_amp).astype(jnp.bfloat16),
        ]
    )


def make_lag_table(col_count):
    flattened = jnp.arange(band_rows * col_count)
    row_of = flattened // col_count
    col_of = flattened % col_count
    lag_lanes = jnp.arange(col_count + band_rows - 1)
    return (lag_lanes[None, :] == (col_of - row_of + band_rows - 1)[:, None]).astype(jnp.bfloat16)


def lag_stack(pair_block, lag_table):
    freq_count, row_count, col_count = pair_block.shape
    group_count = row_count // band_rows
    grouped = pair_block.reshape(freq_count, group_count, band_rows * col_count)
    banded = jnp.einsum("fgk,ku->fgu", grouped, lag_table, preferred_element_type=jnp.float32)
    lag_sums = jnp.zeros((freq_count, col_count + row_count - 1), jnp.float32)
    for row_group in range(group_count):
        first_lag = row_count - band_rows * (row_group + 1)
        lag_sums = lag_sums.at[:, first_lag : first_lag + col_count + band_rows - 1].add(
            banded[:, row_group]
        )
    return lag_sums.T


def correlate(left_rows, right_rows, factor, lag_table):
    left_real = jnp.concatenate([left_rows[0], left_rows[1]], axis=0)
    left_imag = jnp.concatenate([left_rows[1], -left_rows[0]], axis=0)
    right_both = jnp.concatenate([right_rows[0], right_rows[1]], axis=0)
    corr_real = (
        jnp.einsum("wif,wjf->fij", left_real, right_both, preferred_element_type=jnp.float32)
        * factor
    ).astype(jnp.bfloat16)
    corr_imag = (
        jnp.einsum("wif,wjf->fij", left_imag, right_both, preferred_element_type=jnp.float32)
        * factor
    ).astype(jnp.bfloat16)
    return jnp.stack([lag_stack(corr_real, lag_table), lag_stack(corr_imag, lag_table)])


def general_shards(spectra, counts, owners):
    pair_devs = lax.axis_size("pairs")
    member = lax.axis_index("pairs")
    channels = spectra.shape[2]
    half_rows = channels // pair_devs
    source = whiten_rows(spectra)
    receiver = lax.dynamic_slice_in_dim(source, member * half_rows, half_rows, 2)
    block_count = lax.axis_size("cable")
    cable_index = lax.axis_index("cable")
    live_count = jnp.minimum(counts[0], block_count - cable_index)
    panels = {0: receiver}
    for offset in range(1, REACH + 1):
        panels[offset] = from_behind(receiver, "cable", -offset)
    factor = 1.0 / math.sqrt(source.shape[1] * channels)
    lag_table = make_lag_table(half_rows)
    freq_count = source.shape[3]
    stacks = jnp.zeros((2, (REACH + 2) * channels, freq_count), jnp.float32)
    for offset in range(REACH + 1):
        lag_piece = correlate(source, panels[offset], factor, lag_table)
        weight = (offset < live_count).astype(jnp.float32)
        if offset == 0:
            kept_here = weight * lag_piece
        else:
            sent_away = owners[0, offset].astype(jnp.float32)
            arrived = from_behind(weight * sent_away * lag_piece, "cable", offset)
            kept_here = weight * (1.0 - sent_away) * lag_piece + arrived
        first_lag = offset * channels + member * half_rows
        current = lax.dynamic_slice_in_dim(stacks, first_lag, kept_here.shape[1], 1)
        stacks = lax.dynamic_update_slice_in_dim(stacks, current + kept_here, first_lag, 1)
    summed = lax.psum_scatter(stacks, "pairs", scatter_dimension=1, tiled=True)
    return summed[:, None]


EDGE = 128
BAND = 128
GROUP = 4
F32 = jnp.float32
MESH = pl.DeviceIdType.MESH


def channel_transforms(channels, factor):
    points = 2 * channels
    index = np.arange(points)
    angle = 2 * np.pi * np.outer(index, np.arange(channels)) / points
    cos, sin = np.cos(angle), np.sin(angle)
    full = np.block([[cos, sin], [-sin, cos]])
    high = full.astype(jnp.bfloat16)
    low = (full - high.astype(np.float64)).astype(jnp.bfloat16)
    forward = np.concatenate([high, low], axis=1)
    angle = 2 * np.pi * np.outer(index - (channels - 1), index) / points
    cos, sin = np.cos(angle), np.sin(angle)
    cos[-1], sin[-1] = 0.0, 0.0
    inverse = np.block([[cos, sin], [-sin, cos]]) * (factor / points)
    return jnp.asarray(forward), jnp.asarray(inverse.astype(np.float32))


def stack_kernel(
    spectra_ref, counts_ref, owners_ref, forward_ref, inverse_ref, out_ref,
    x_ref, flag_ref, white, far, back, spec, other, sums, sums_back, stack, piece_out, piece_back, piece_in, arrived, swapped, seen,
    chain_send, chain_recv, back_send, back_recv, piece_send, piece_recv,
    next_send, next_recv, swap_send, swap_recv, flag_send, flag_recv, load_sem, edge_send, edge_recv,
):
    windows, channels = x_ref.shape[1:3]
    half = x_ref.shape[3] - 2 * EDGE
    bands, groups = half // BAND, windows // GROUP
    points = 2 * channels
    kept = out_ref.shape[1]
    blocks, halves = lax.axis_size("cable"), lax.axis_size("pairs")
    z, m = lax.axis_index("cable"), lax.axis_index("pairs")
    cuts, x = lax.axis_size("bins"), lax.axis_index("bins")
    bins = spectra_ref.shape[3]
    first = m == 0
    mirrored = jnp.where((x > 0) & (first | (x == cuts - 1)), 1, 0)
    onward = {"cable": lax.rem(z + 1, blocks)}
    backward = {"cable": lax.rem(z + blocks - 1, blocks)}
    partner = {"pairs": lax.rem(m + 1, halves)}

    def remote(source, target, send, recv, device):
        return pltpu.make_async_remote_copy(
            src_ref=source, dst_ref=target, send_sem=send, recv_sem=recv, device_id=device, device_id_type=MESH
        )

    def first_hop(s):
        return remote(white.at[s], far.at[s], chain_send.at[s], chain_recv.at[s], onward)

    def next_hop(s):
        return remote(far.at[s], far.at[s], chain_send.at[s], chain_recv.at[s], onward)

    def back_hop(s):
        return remote(white.at[s], back.at[s], back_send.at[s], back_recv.at[s], backward)

    def to_first(c, slot):
        return remote(piece_out.at[c], piece_in.at[slot, c], piece_send.at[c], piece_recv.at[slot, c], {"cable": 0})

    def to_next(c):
        return remote(piece_back.at[c], arrived.at[c], next_send.at[c], next_recv.at[c], onward)

    def swap(c):
        rows = pl.ds(pl.multiple_of((1 - m) * kept, 8), kept)
        return remote(
            stack.at[c, :, rows], swapped.at[place(c)], swap_send.at[c], swap_recv.at[place(c)], partner
        )

    def place(c):
        return c + mirrored * (bands - 1 - 2 * c)

    def load(q):
        near = pl.multiple_of(m * (half - EDGE), EDGE)
        spot = pl.multiple_of((1 - m) * EDGE, EDGE)
        rows = pl.ds(q * GROUP, GROUP)
        return pltpu.make_async_copy(
            spectra_ref.at[:, rows, :, pl.ds(near, half + EDGE)],
            x_ref.at[:, rows, :, pl.ds(spot, half + EDGE)],
            load_sem.at[q],
        )

    spot = pl.ds(pl.multiple_of(m * (half + EDGE), EDGE), EDGE)

    def edge():
        source = pl.ds(pl.multiple_of((1 - m) * (bins - EDGE), EDGE), EDGE)
        target = {"bins": lax.rem(x + cuts + 1 - 2 * m, cuts)}
        return remote(
            spectra_ref.at[:, :, :, source], x_ref.at[:, :, :, spot], edge_send.at[0], edge_recv.at[0], target
        )

    def flags_to(block):
        return remote(flag_ref, seen, flag_send.at[block - 1], flag_recv.at[0], {"cable": block})

    for q in range(groups):
        load(q).start()
    live = jnp.minimum(counts_ref[0], blocks - z)
    for offset in range(REACH + 1):
        flag_ref[offset : offset + 1, :] = jnp.full((1, BAND), owners_ref[0, offset].astype(F32))
        weight = jnp.where(offset < live, 1.0, 0.0)
        flag_ref[REACH + 1 + offset : REACH + 2 + offset, :] = jnp.full((1, BAND), weight)
    barrier = pltpu.get_barrier_semaphore()
    for step in range(1, blocks):
        pl.semaphore_signal(barrier, inc=1, device_id={"cable": lax.rem(z + step, blocks)}, device_id_type=MESH)
    pl.semaphore_signal(barrier, inc=1, device_id=partner, device_id_type=MESH)
    for step in range(1, cuts):
        pl.semaphore_signal(barrier, inc=1, device_id={"bins": lax.rem(x + step, cuts)}, device_id_type=MESH)
    pl.semaphore_wait(barrier, blocks + cuts - 1)
    sends_edge = (first & (x < cuts - 1)) | (~first & (x > 0))
    takes_edge = (first & (x > 0)) | (~first & (x < cuts - 1))

    @pl.when(sends_edge)
    def _():
        edge().start()

    @pl.when(~takes_edge)
    def _():
        x_ref[:, :, :, spot] = jnp.zeros((2, windows, channels, EDGE), x_ref.dtype)


    @pl.when(z == 0)
    def _():
        for block in range(1, blocks):
            flags_to(block).start()

    def whiten(q, begin, count, store):
        length = count * BAND + 2 * EDGE
        lanes = pl.ds(pl.multiple_of(begin, BAND), length)
        for i in range(GROUP):
            real = x_ref[0, q * GROUP + i, :, lanes].astype(F32)
            imag = x_ref[1, q * GROUP + i, :, lanes].astype(F32)
            power = real * real + imag * imag
            total, width = power, 1
            while width < 2 * HALF_WIDTH:
                total = total + pltpu.roll(total, width, 1)
                width *= 2
            total = total + pltpu.roll(power, width, 1)
            total = pltpu.roll(total, length - HALF_WIDTH, 1)[:, EDGE : length - EDGE]
            gain = lax.rsqrt(total / (2 * HALF_WIDTH + 1) + epsilon)
            real = (real[:, EDGE : length - EDGE] * gain).astype(jnp.bfloat16)
            imag = (imag[:, EDGE : length - EDGE] * gain).astype(jnp.bfloat16)
            for j in range(count):
                slot = store(j) * groups + q
                white[slot, i, :channels] = real[:, j * BAND : (j + 1) * BAND]
                white[slot, i, channels:] = imag[:, j * BAND : (j + 1) * BAND]

    def whiten_inner(q, carry):
        load(q).wait()
        whiten(q, mirrored * BAND, bands - 1, lambda j: j + mirrored * (bands - 2 - 2 * j))

        @pl.when(z == 0)
        def _():
            first_hop(q).start()

        @pl.when(z == blocks - 1)
        def _():
            back_hop(q).start()

        return carry

    def whiten_last(q, carry):
        whiten(q, (1 - mirrored) * (bands - 1) * BAND, 1, lambda j: bands - 1)
        s = (bands - 1) * groups + q

        @pl.when(z == 0)
        def _():
            first_hop(s).start()

        @pl.when(z == blocks - 1)
        def _():
            back_hop(s).start()

        return carry

    lax.fori_loop(0, groups, whiten_inner, 0)

    @pl.when(z == 0)
    def _():
        @pl.loop(groups, (bands - 1) * groups)
        def _(s):
            first_hop(s).start()

    @pl.when(z == blocks - 1)
    def _():
        @pl.loop(groups, (bands - 1) * groups)
        def _(s):
            back_hop(s).start()

    @pl.when(takes_edge)
    def _():
        edge().wait_recv()

    lax.fori_loop(0, groups, whiten_last, 0)

    def transform(buffer, s):
        wide = jnp.concatenate([buffer[s, i] for i in range(GROUP)], axis=1)
        return jnp.dot(forward_ref[...], jnp.concatenate([wide, wide], axis=0), preferred_element_type=F32)

    tile = 32

    def power_into(total, s):
        for k in range(0, points, tile):
            gained = total[k : k + tile]
            for i in range(GROUP):
                lanes = slice(i * BAND, (i + 1) * BAND)
                real = spec[s, k : k + tile, lanes]
                imag = spec[s, points + k : points + k + tile, lanes]
                gained = gained + (real * real + imag * imag)
            total[k : k + tile] = gained

    def cross_into(total, s, sign):
        for k in range(0, points, tile):
            gained_real = total[k : k + tile]
            gained_imag = total[points + k : points + k + tile]
            for i in range(GROUP):
                lanes = slice(i * BAND, (i + 1) * BAND)
                own_real = spec[s, k : k + tile, lanes]
                own_imag = spec[s, points + k : points + k + tile, lanes]
                real = other[k : k + tile, lanes]
                imag = other[points + k : points + k + tile, lanes]
                gained_real = gained_real + (own_real * real + own_imag * imag)
                if sign > 0:
                    gained_imag = gained_imag + (own_imag * real - own_real * imag)
                else:
                    gained_imag = gained_imag + (own_real * imag - own_imag * real)
            total[k : k + tile] = gained_real
            total[points + k : points + k + tile] = gained_imag

    def lags_of(values, columns):
        return jnp.dot(
            inverse_ref[:, :columns], values, preferred_element_type=F32, precision=lax.Precision.HIGHEST
        )

    def add_piece(c, first, piece):
        rows = pl.ds(first, points)
        stack[c, 0, rows] += piece[:points]
        stack[c, 1, rows] += piece[points:]

    def own_band(c, carry):
        sums[...] = jnp.zeros_like(sums)

        def step(q, inner):
            s = c * groups + q
            spec[s] = transform(white, s)
            power_into(sums, s)
            return inner

        lax.fori_loop(0, groups, step, 0)
        stack[c] = jnp.zeros(stack.shape[1:], F32)
        add_piece(c, 0, flag_ref[REACH + 1 : REACH + 2, :] * lags_of(sums[:points], points))
        return carry

    lax.fori_loop(0, bands, own_band, 0)

    @pl.when(z > 0)
    def _():
        flags_to(1).wait_recv()

        def far_band(c, carry):
            sums[...] = jnp.zeros_like(sums)
            sums_back[...] = jnp.zeros_like(sums_back)

            def step(q, inner):
                s = c * groups + q
                next_hop(s).wait_recv()

                @pl.when(z < blocks - 1)
                def _():
                    next_hop(s).start()

                other[...] = transform(far, s)
                cross_into(sums, s, -1)

                @pl.when(z == blocks - 2)
                def _():
                    back_hop(s).wait_recv()
                    other[...] = transform(back, s)
                    cross_into(sums_back, s, 1)

                return inner

            lax.fori_loop(0, groups, step, 0)
            piece = lags_of(sums[...], 2 * points)
            piece_out[c] = piece
            to_first(c, z - 1).start()
            counted = seen[pl.ds(z, 1), :] * seen[pl.ds(REACH + 1 + z, 1), :]
            add_piece(c, pl.multiple_of(z * channels, 8), counted * piece)

            @pl.when(z == blocks - 2)
            def _():
                piece = flag_ref[REACH + 2 : REACH + 3, :] * lags_of(sums_back[...], 2 * points)
                sent = flag_ref[1:2, :]
                piece_back[c] = sent * piece
                to_next(c).start()
                add_piece(c, channels, (1.0 - sent) * piece)

            @pl.when(z == blocks - 1)
            def _():
                to_next(c).wait_recv()
                add_piece(c, channels, arrived[c])

            swap(c).start()
            return carry

        lax.fori_loop(0, bands, far_band, 0)

    @pl.when(z == 0)
    def _():
        def near_band(c, carry):
            for offset in range(1, blocks):
                to_first(c, offset - 1).wait_recv()
                counted = (1.0 - flag_ref[offset : offset + 1, :]) * flag_ref[REACH + 1 + offset : REACH + 2 + offset, :]
                add_piece(c, offset * channels, counted * piece_in[offset - 1, c])
            swap(c).start()
            return carry

        lax.fori_loop(0, bands, near_band, 0)

    def collect(c, carry):
        mine = pl.ds(pl.multiple_of(m * half + place(c) * BAND, BAND), BAND)
        theirs = pl.ds(pl.multiple_of((1 - m) * half + place(c) * BAND, BAND), BAND)
        out_ref[:, :, mine] = stack[c, :, pl.ds(pl.multiple_of(m * kept, 8), kept)]
        swap(c).wait_recv()
        out_ref[:, :, theirs] = swapped[place(c)]
        swap(c).wait_send()
        return carry

    lax.fori_loop(0, bands, collect, 0)

    @pl.when(sends_edge)
    def _():
        edge().wait_send()

    @pl.when(z < blocks - 1)
    def _():
        @pl.loop(0, bands * groups)
        def _(s):
            next_hop(s).wait_send()

    @pl.when(z == blocks - 1)
    def _():
        @pl.loop(0, bands * groups)
        def _(s):
            back_hop(s).wait_send()

    @pl.when(z > 0)
    def _():
        @pl.loop(0, bands)
        def _(c):
            to_first(c, z - 1).wait_send()

    @pl.when(z == blocks - 2)
    def _():
        @pl.loop(0, bands)
        def _(c):
            to_next(c).wait_send()

    @pl.when(z == 0)
    def _():
        for block in range(1, blocks):
            flags_to(block).wait_send()


def four_block_shards(spectra, counts, owners):
    parts, windows, channels, bins = spectra.shape
    halves, blocks = lax.axis_size("pairs"), lax.axis_size("cable")
    half, points = bins // halves, 2 * channels
    forward, inverse = channel_transforms(channels, 1.0 / math.sqrt(windows * channels))
    bands, groups = half // BAND, windows // GROUP
    pieces = bands * groups
    rows = (REACH + 2) * channels
    kept = rows // halves
    block = pltpu.VMEM((pieces, GROUP, points, BAND), jnp.bfloat16)
    lags = pltpu.VMEM((bands, 2 * points, BAND), F32)
    dma = pltpu.SemaphoreType.DMA
    out = pl.pallas_call(
        stack_kernel,
        out_shape=jax.ShapeDtypeStruct((2, kept, bins), F32),
        in_specs=[
            pl.BlockSpec(memory_space=pl.ANY),
            pl.BlockSpec(memory_space=pltpu.SMEM),
            pl.BlockSpec(memory_space=pltpu.SMEM),
            pl.BlockSpec(memory_space=pltpu.VMEM),
            pl.BlockSpec(memory_space=pltpu.VMEM),
        ],
        out_specs=pl.BlockSpec(memory_space=pltpu.VMEM),
        scratch_shapes=[
            pltpu.VMEM((2, windows, channels, half + 2 * EDGE), jnp.bfloat16),
            pltpu.VMEM((2 * (REACH + 1), BAND), F32),
            block, block, block,
            pltpu.VMEM((pieces, 2 * points, GROUP * BAND), F32),
            pltpu.VMEM((2 * points, GROUP * BAND), F32),
            pltpu.VMEM((2 * points, BAND), F32),
            pltpu.VMEM((2 * points, BAND), F32),
            pltpu.VMEM((bands, 2, rows, BAND), F32),
            lags, lags,
            pltpu.VMEM((blocks - 1, bands, 2 * points, BAND), F32),
            lags,
            pltpu.VMEM((bands, 2, kept, BAND), F32),
            pltpu.VMEM((2 * (REACH + 1), BAND), F32),
            dma((pieces,)), dma((pieces,)), dma((pieces,)), dma((pieces,)),
            dma((bands,)), dma((blocks - 1, bands)),
            dma((bands,)), dma((bands,)), dma((bands,)), dma((bands,)),
            dma((blocks - 1,)), dma((1,)),
            dma((groups,)), dma((1,)), dma((1,)),
        ],
        compiler_params=pltpu.CompilerParams(
            collective_id=0, has_side_effects=True, vmem_limit_bytes=60 * 1024 * 1024
        ),
    )(spectra, counts, owners, forward, inverse)
    return out[:, None]


def solution(mesh):
    sizes = dict(mesh.shape)
    fits = sizes["cable"] == REACH + 1 and sizes["pairs"] == 2
    shards = four_block_shards if fits else general_shards
    placed = (
        P("groups", None, "cable", "bins"),
        P(("groups", "cable")),
        P(("groups", "cable"), None),
    )
    return jax.shard_map(
        shards,
        mesh=mesh,
        in_specs=placed,
        out_specs=P("groups", "cable", "pairs", "bins"),
        check_vma=False,
    )
```

```python
import math

import jax
import jax.numpy as jnp
import numpy as np
from jax import lax
from jax.experimental import pallas as pl
from jax.experimental.pallas import tpu as pltpu
from jax.sharding import PartitionSpec as P

REACH = 3
HALF_WIDTH = 32


epsilon = 1e-06
band_rows = 16


def with_halo(x, sides, width):
    for axis, dim in sides:
        count, length = (lax.axis_size(axis), x.shape[dim])
        up = [(i, (i + 1) % count) for i in range(count - 1)]
        down = [(j, i) for i, j in up]
        last = lax.slice_in_dim(x, length - width, length, axis=dim)
        first = lax.slice_in_dim(x, 0, width, axis=dim)
        before = lax.ppermute(last, axis, up)
        after = lax.ppermute(first, axis, down)
        x = jnp.concatenate([before, x, after], axis=dim)
    return x


def from_behind(block, axis, distance):
    devices = range(lax.axis_size(axis))
    route = [(i - distance, i) for i in devices if i - distance in devices]
    return lax.ppermute(block, axis, route)


def whiten_rows(spectra):
    real_part = spectra[0].astype(jnp.float32)
    imag_part = spectra[1].astype(jnp.float32)
    power_sum = real_part * real_part + imag_part * imag_part
    padded = with_halo(power_sum, (("bins", 2),), HALF_WIDTH)
    window_len = 2 * HALF_WIDTH + 1
    window_sum = lax.reduce_window(
        padded, jnp.zeros((), padded.dtype), lax.add, (1, 1, window_len), (1, 1, 1), "VALID"
    )
    inverse_amp = lax.rsqrt(window_sum / window_len + epsilon)
    return jnp.stack(
        [
            (real_part * inverse_amp).astype(jnp.bfloat16),
            (imag_part * inverse_amp).astype(jnp.bfloat16),
        ]
    )


def make_lag_table(col_count):
    flattened = jnp.arange(band_rows * col_count)
    row_of = flattened // col_count
    col_of = flattened % col_count
    lag_lanes = jnp.arange(col_count + band_rows - 1)
    return (lag_lanes[None, :] == (col_of - row_of + band_rows - 1)[:, None]).astype(jnp.bfloat16)


def lag_stack(pair_block, lag_table):
    freq_count, row_count, col_count = pair_block.shape
    group_count = row_count // band_rows
    grouped = pair_block.reshape(freq_count, group_count, band_rows * col_count)
    banded = jnp.einsum("fgk,ku->fgu", grouped, lag_table, preferred_element_type=jnp.float32)
    lag_sums = jnp.zeros((freq_count, col_count + row_count - 1), jnp.float32)
    for row_group in range(group_count):
        first_lag = row_count - band_rows * (row_group + 1)
        lag_sums = lag_sums.at[:, first_lag : first_lag + col_count + band_rows - 1].add(
            banded[:, row_group]
        )
    return lag_sums.T


def correlate(left_rows, right_rows, factor, lag_table):
    left_real = jnp.concatenate([left_rows[0], left_rows[1]], axis=0)
    left_imag = jnp.concatenate([left_rows[1], -left_rows[0]], axis=0)
    right_both = jnp.concatenate([right_rows[0], right_rows[1]], axis=0)
    corr_real = (
        jnp.einsum("wif,wjf->fij", left_real, right_both, preferred_element_type=jnp.float32)
        * factor
    ).astype(jnp.bfloat16)
    corr_imag = (
        jnp.einsum("wif,wjf->fij", left_imag, right_both, preferred_element_type=jnp.float32)
        * factor
    ).astype(jnp.bfloat16)
    return jnp.stack([lag_stack(corr_real, lag_table), lag_stack(corr_imag, lag_table)])


def general_shards(spectra, counts, owners):
    pair_devs = lax.axis_size("pairs")
    member = lax.axis_index("pairs")
    channels = spectra.shape[2]
    half_rows = channels // pair_devs
    source = whiten_rows(spectra)
    receiver = lax.dynamic_slice_in_dim(source, member * half_rows, half_rows, 2)
    block_count = lax.axis_size("cable")
    cable_index = lax.axis_index("cable")
    live_count = jnp.minimum(counts[0], block_count - cable_index)
    panels = {0: receiver}
    for offset in range(1, REACH + 1):
        panels[offset] = from_behind(receiver, "cable", -offset)
    factor = 1.0 / math.sqrt(source.shape[1] * channels)
    lag_table = make_lag_table(half_rows)
    freq_count = source.shape[3]
    stacks = jnp.zeros((2, (REACH + 2) * channels, freq_count), jnp.float32)
    for offset in range(REACH + 1):
        lag_piece = correlate(source, panels[offset], factor, lag_table)
        weight = (offset < live_count).astype(jnp.float32)
        if offset == 0:
            kept_here = weight * lag_piece
        else:
            sent_away = owners[0, offset].astype(jnp.float32)
            arrived = from_behind(weight * sent_away * lag_piece, "cable", offset)
            kept_here = weight * (1.0 - sent_away) * lag_piece + arrived
        first_lag = offset * channels + member * half_rows
        current = lax.dynamic_slice_in_dim(stacks, first_lag, kept_here.shape[1], 1)
        stacks = lax.dynamic_update_slice_in_dim(stacks, current + kept_here, first_lag, 1)
    summed = lax.psum_scatter(stacks, "pairs", scatter_dimension=1, tiled=True)
    return summed[:, None]


EDGE = 128
BAND = 128
GROUP = 2
EARLY = 2
F32 = jnp.float32
MESH = pl.DeviceIdType.MESH


def channel_transforms(channels, factor):
    points = 2 * channels
    index = np.arange(points)
    angle = 2 * np.pi * np.outer(index, np.arange(channels)) / points
    cos, sin = np.cos(angle), np.sin(angle)
    full = np.block([[cos, sin], [-sin, cos]])
    high = full.astype(jnp.bfloat16)
    low = (full - high.astype(np.float64)).astype(jnp.bfloat16)
    forward = np.concatenate([high, low], axis=1)
    angle = 2 * np.pi * np.outer(index - (channels - 1), index) / points
    cos, sin = np.cos(angle), np.sin(angle)
    cos[-1], sin[-1] = 0.0, 0.0
    inverse = np.block([[cos, sin], [-sin, cos]]) * (factor / points)
    return jnp.asarray(forward), jnp.asarray(inverse.astype(np.float32))


def stack_kernel(
    spectra_ref, counts_ref, owners_ref, forward_ref, inverse_ref, out_ref,
    x_ref, flag_ref, white, far, back, spec, other, third, sums, sums_back, sums_far, stack, piece_out, piece_back, piece_in, arrived, swapped, seen,
    chain_send, chain_recv, back_send, back_recv, piece_send, piece_recv,
    next_send, next_recv, swap_send, swap_recv, flag_send, flag_recv, load_sem, edge_send, edge_recv,
):
    windows, channels = x_ref.shape[1:3]
    half = x_ref.shape[3] - 2 * EDGE
    bands, groups = half // BAND, windows // GROUP
    points = 2 * channels
    kept = out_ref.shape[1]
    blocks, halves = lax.axis_size("cable"), lax.axis_size("pairs")
    z, m = lax.axis_index("cable"), lax.axis_index("pairs")
    cuts, x = lax.axis_size("bins"), lax.axis_index("bins")
    bins = spectra_ref.shape[3]
    first = m == 0
    mirrored = jnp.where((x > 0) & (first | (x == cuts - 1)), 1, 0)
    onward = {"cable": lax.rem(z + 1, blocks)}
    backward = {"cable": lax.rem(z + blocks - 1, blocks)}
    partner = {"pairs": lax.rem(m + 1, halves)}

    def remote(source, target, send, recv, device):
        return pltpu.make_async_remote_copy(
            src_ref=source, dst_ref=target, send_sem=send, recv_sem=recv, device_id=device, device_id_type=MESH
        )

    def first_hop(s):
        return remote(white.at[s], far.at[s], chain_send.at[s], chain_recv.at[s], onward)

    def next_hop(s):
        return remote(far.at[s], far.at[s], chain_send.at[s], chain_recv.at[s], onward)

    def back_hop(s):
        return remote(white.at[s], back.at[s], back_send.at[s], back_recv.at[s], backward)

    def to_first(c, kind, slot):
        return remote(
            piece_out.at[kind, c], piece_in.at[slot, c], piece_send.at[kind, c], piece_recv.at[slot, c], {"cable": 0}
        )

    def to_next(c):
        return remote(piece_back.at[c], arrived.at[c], next_send.at[c], next_recv.at[c], onward)

    def swap(c):
        rows = pl.ds(pl.multiple_of((1 - m) * kept, 8), kept)
        return remote(
            stack.at[c, :, rows], swapped.at[place(c)], swap_send.at[c], swap_recv.at[place(c)], partner
        )

    def place(c):
        return c + mirrored * (bands - 1 - 2 * c)

    def load(q):
        near = pl.multiple_of(m * (half - EDGE), EDGE)
        spot = pl.multiple_of((1 - m) * EDGE, EDGE)
        rows = pl.ds(q * GROUP, GROUP)
        return pltpu.make_async_copy(
            spectra_ref.at[:, rows, :, pl.ds(near, half + EDGE)],
            x_ref.at[:, rows, :, pl.ds(spot, half + EDGE)],
            load_sem.at[q],
        )

    spot = pl.ds(pl.multiple_of(m * (half + EDGE), EDGE), EDGE)

    def edge():
        source = pl.ds(pl.multiple_of((1 - m) * (bins - EDGE), EDGE), EDGE)
        target = {"bins": lax.rem(x + cuts + 1 - 2 * m, cuts)}
        return remote(
            spectra_ref.at[:, :, :, source], x_ref.at[:, :, :, spot], edge_send.at[0], edge_recv.at[0], target
        )

    def flags_to(block):
        return remote(flag_ref, seen, flag_send.at[block - 1], flag_recv.at[0], {"cable": block})

    for q in range(groups):
        load(q).start()
    live = jnp.minimum(counts_ref[0], blocks - z)
    for offset in range(REACH + 1):
        flag_ref[offset : offset + 1, :] = jnp.full((1, BAND), owners_ref[0, offset].astype(F32))
        weight = jnp.where(offset < live, 1.0, 0.0)
        flag_ref[REACH + 1 + offset : REACH + 2 + offset, :] = jnp.full((1, BAND), weight)
    barrier = pltpu.get_barrier_semaphore()
    for step in range(1, blocks):
        pl.semaphore_signal(barrier, inc=1, device_id={"cable": lax.rem(z + step, blocks)}, device_id_type=MESH)
    pl.semaphore_signal(barrier, inc=1, device_id=partner, device_id_type=MESH)
    for step in range(1, cuts):
        pl.semaphore_signal(barrier, inc=1, device_id={"bins": lax.rem(x + step, cuts)}, device_id_type=MESH)
    pl.semaphore_wait(barrier, blocks + cuts - 1)
    sends_edge = (first & (x < cuts - 1)) | (~first & (x > 0))
    takes_edge = (first & (x > 0)) | (~first & (x < cuts - 1))

    @pl.when(sends_edge)
    def _():
        edge().start()

    @pl.when(~takes_edge)
    def _():
        x_ref[:, :, :, spot] = jnp.zeros((2, windows, channels, EDGE), x_ref.dtype)


    @pl.when(z == 0)
    def _():
        for block in range(1, blocks - 1):
            flags_to(block).start()

    def whiten(q, begin, count, store):
        length = count * BAND + 2 * EDGE
        lanes = pl.ds(pl.multiple_of(begin, BAND), length)
        for i in range(GROUP):
            real = x_ref[0, q * GROUP + i, :, lanes].astype(F32)
            imag = x_ref[1, q * GROUP + i, :, lanes].astype(F32)
            power = real * real + imag * imag
            total, width = power, 1
            while width < 2 * HALF_WIDTH:
                total = total + pltpu.roll(total, width, 1)
                width *= 2
            total = total + pltpu.roll(power, width, 1)
            total = pltpu.roll(total, length - HALF_WIDTH, 1)[:, EDGE : length - EDGE]
            gain = lax.rsqrt(total / (2 * HALF_WIDTH + 1) + epsilon)
            real = (real[:, EDGE : length - EDGE] * gain).astype(jnp.bfloat16)
            imag = (imag[:, EDGE : length - EDGE] * gain).astype(jnp.bfloat16)
            for j in range(count):
                slot = store(j) * groups + q
                white[slot, i, :channels] = real[:, j * BAND : (j + 1) * BAND]
                white[slot, i, channels:] = imag[:, j * BAND : (j + 1) * BAND]

    def whiten_inner(q, carry):
        load(q).wait()
        whiten(q, mirrored * BAND, bands - 1, lambda j: j + mirrored * (bands - 2 - 2 * j))

        @pl.when(z == 0)
        def _():
            first_hop(q).start()

        @pl.when(z == blocks - 1)
        def _():
            back_hop(q).start()

        return carry

    def whiten_last(q, carry):
        whiten(q, (1 - mirrored) * (bands - 1) * BAND, 1, lambda j: bands - 1)
        s = (bands - 1) * groups + q

        @pl.when(z == 0)
        def _():
            first_hop(s).start()

        @pl.when(z == blocks - 1)
        def _():
            back_hop(s).start()

        return carry

    def relay(s):
        next_hop(s).wait_recv()
        next_hop(s).start()

    def relay_early(stage):
        @pl.when(z == 1)
        def _():
            for k in range(EARLY):
                relay(stage * EARLY + k)

    lax.fori_loop(0, groups, whiten_inner, 0)
    relay_early(0)

    @pl.when(z == 0)
    def _():
        @pl.loop(groups, (bands - 1) * groups)
        def _(s):
            first_hop(s).start()

    @pl.when(z == blocks - 1)
    def _():
        @pl.loop(groups, (bands - 1) * groups)
        def _(s):
            back_hop(s).start()

    @pl.when(takes_edge)
    def _():
        edge().wait_recv()

    lax.fori_loop(0, groups, whiten_last, 0)
    relay_early(1)

    def transform(buffer, s):
        wide = jnp.concatenate([buffer[s, i] for i in range(GROUP)], axis=1)
        return jnp.dot(forward_ref[...], jnp.concatenate([wide, wide], axis=0), preferred_element_type=F32)

    tile = 32

    def power_into(total, s):
        for k in range(0, points, tile):
            gained = total[k : k + tile]
            for i in range(GROUP):
                lanes = slice(i * BAND, (i + 1) * BAND)
                real = spec[s, k : k + tile, lanes]
                imag = spec[s, points + k : points + k + tile, lanes]
                gained = gained + (real * real + imag * imag)
            total[k : k + tile] = gained

    def cross_into(total, near, far):
        for k in range(0, points, tile):
            gained_real = total[k : k + tile]
            gained_imag = total[points + k : points + k + tile]
            for i in range(GROUP):
                lanes = slice(i * BAND, (i + 1) * BAND)
                near_real = near[k : k + tile, lanes]
                near_imag = near[points + k : points + k + tile, lanes]
                far_real = far[k : k + tile, lanes]
                far_imag = far[points + k : points + k + tile, lanes]
                gained_real = gained_real + (near_real * far_real + near_imag * far_imag)
                gained_imag = gained_imag + (near_imag * far_real - near_real * far_imag)
            total[k : k + tile] = gained_real
            total[points + k : points + k + tile] = gained_imag

    def lags_of(values, columns):
        return jnp.dot(
            inverse_ref[:, :columns], values, preferred_element_type=F32, precision=lax.Precision.HIGHEST
        )

    def add_piece(c, first, piece):
        rows = pl.ds(first, points)
        stack[c, 0, rows] += piece[:points]
        stack[c, 1, rows] += piece[points:]

    def own_band(c, carry):
        sums[...] = jnp.zeros_like(sums)

        def step(q, inner):
            s = c * groups + q
            spec[s] = transform(white, s)
            power_into(sums, s)
            return inner

        lax.fori_loop(0, groups, step, 0)
        stack[c] = jnp.zeros(stack.shape[1:], F32)
        add_piece(c, 0, flag_ref[REACH + 1 : REACH + 2, :] * lags_of(sums[:points], points))
        return carry

    lax.fori_loop(0, bands, own_band, 0)
    relay_early(2)

    def counted_far(offset):
        return seen[offset : offset + 1, :] * seen[REACH + 1 + offset : REACH + 2 + offset, :]

    @pl.when(z == 1)
    def _():
        flags_to(1).wait_recv()

        def band(c, carry):
            sums[...] = jnp.zeros_like(sums)

            def step(q, inner):
                s = c * groups + q

                @pl.when(s >= 3 * EARLY)
                def _():
                    relay(s)

                other[...] = transform(far, s)
                cross_into(sums, other, spec.at[s])
                return inner

            lax.fori_loop(0, groups, step, 0)
            piece = lags_of(sums[...], 2 * points)
            piece_out[0, c] = piece.astype(piece_out.dtype)
            to_first(c, 0, 0).start()
            add_piece(c, channels, counted_far(1) * piece)
            swap(c).start()
            return carry

        lax.fori_loop(0, bands, band, 0)

    @pl.when(z == 2)
    def _():
        flags_to(1).wait_recv()

        def band(c, carry):
            sums[...] = jnp.zeros_like(sums)
            sums_back[...] = jnp.zeros_like(sums_back)
            sums_far[...] = jnp.zeros_like(sums_far)

            def step(q, inner):
                s = c * groups + q
                back_hop(s).wait_recv()
                third[...] = transform(back, s)
                cross_into(sums_back, spec.at[s], third)
                next_hop(s).wait_recv()
                other[...] = transform(far, s)
                cross_into(sums, other, spec.at[s])
                cross_into(sums_far, other, third)
                return inner

            lax.fori_loop(0, groups, step, 0)
            piece = lags_of(sums[...], 2 * points)
            piece_out[0, c] = piece.astype(piece_out.dtype)
            to_first(c, 0, 1).start()
            distant = lags_of(sums_far[...], 2 * points)
            piece_out[1, c] = distant.astype(piece_out.dtype)
            to_first(c, 1, 2).start()
            ahead = flag_ref[REACH + 2 : REACH + 3, :] * lags_of(sums_back[...], 2 * points)
            sent = flag_ref[1:2, :]
            piece_back[c, 0] = (sent * ahead).astype(piece_back.dtype)
            piece_back[c, 1] = (counted_far(3) * distant).astype(piece_back.dtype)
            to_next(c).start()
            add_piece(c, 2 * channels, counted_far(2) * piece)
            add_piece(c, channels, (1.0 - sent) * ahead)
            swap(c).start()
            return carry

        lax.fori_loop(0, bands, band, 0)

    @pl.when(z == blocks - 1)
    def _():
        def band(c, carry):
            to_next(c).wait_recv()
            add_piece(c, channels, arrived[c, 0].astype(F32))
            add_piece(c, 3 * channels, arrived[c, 1].astype(F32))
            swap(c).start()
            return carry

        lax.fori_loop(0, bands, band, 0)

    @pl.when(z == 0)
    def _():
        def band(c, carry):
            for offset in range(1, blocks):
                to_first(c, 0, offset - 1).wait_recv()
                counted = (1.0 - flag_ref[offset : offset + 1, :]) * flag_ref[REACH + 1 + offset : REACH + 2 + offset, :]
                add_piece(c, offset * channels, counted * piece_in[offset - 1, c].astype(F32))
            swap(c).start()
            return carry

        lax.fori_loop(0, bands, band, 0)

    def collect(c, carry):
        mine = pl.ds(pl.multiple_of(m * half + place(c) * BAND, BAND), BAND)
        theirs = pl.ds(pl.multiple_of((1 - m) * half + place(c) * BAND, BAND), BAND)
        out_ref[:, :, mine] = stack[c, :, pl.ds(pl.multiple_of(m * kept, 8), kept)]
        swap(c).wait_recv()
        out_ref[:, :, theirs] = swapped[place(c)]
        swap(c).wait_send()
        return carry

    lax.fori_loop(0, bands, collect, 0)

    @pl.when(sends_edge)
    def _():
        edge().wait_send()

    @pl.when(z < 2)
    def _():
        @pl.loop(0, bands * groups)
        def _(s):
            next_hop(s).wait_send()

    @pl.when(z == blocks - 1)
    def _():
        @pl.loop(0, bands * groups)
        def _(s):
            back_hop(s).wait_send()

    @pl.when((z == 1) | (z == 2))
    def _():
        @pl.loop(0, bands)
        def _(c):
            to_first(c, 0, z - 1).wait_send()

    @pl.when(z == 2)
    def _():
        @pl.loop(0, bands)
        def _(c):
            to_first(c, 1, 2).wait_send()
            to_next(c).wait_send()

    @pl.when(z == 0)
    def _():
        for block in range(1, blocks - 1):
            flags_to(block).wait_send()


def four_block_shards(spectra, counts, owners):
    parts, windows, channels, bins = spectra.shape
    halves, blocks = lax.axis_size("pairs"), lax.axis_size("cable")
    half, points = bins // halves, 2 * channels
    forward, inverse = channel_transforms(channels, 1.0 / math.sqrt(windows * channels))
    bands, groups = half // BAND, windows // GROUP
    pieces = bands * groups
    rows = (REACH + 2) * channels
    kept = rows // halves
    block = pltpu.VMEM((pieces, GROUP, points, BAND), jnp.bfloat16)
    spectrum = pltpu.VMEM((2 * points, GROUP * BAND), F32)
    sums = pltpu.VMEM((2 * points, BAND), F32)

    def lags(lead):
        return pltpu.VMEM(lead + (2 * points, BAND), jnp.bfloat16)

    dma = pltpu.SemaphoreType.DMA
    out = pl.pallas_call(
        stack_kernel,
        out_shape=jax.ShapeDtypeStruct((2, kept, bins), F32),
        in_specs=[
            pl.BlockSpec(memory_space=pl.ANY),
            pl.BlockSpec(memory_space=pltpu.SMEM),
            pl.BlockSpec(memory_space=pltpu.SMEM),
            pl.BlockSpec(memory_space=pltpu.VMEM),
            pl.BlockSpec(memory_space=pltpu.VMEM),
        ],
        out_specs=pl.BlockSpec(memory_space=pltpu.VMEM),
        scratch_shapes=[
            pltpu.VMEM((2, windows, channels, half + 2 * EDGE), jnp.bfloat16),
            pltpu.VMEM((2 * (REACH + 1), BAND), F32),
            block, block, block,
            pltpu.VMEM((pieces, 2 * points, GROUP * BAND), F32),
            spectrum, spectrum, sums, sums, sums,
            pltpu.VMEM((bands, 2, rows, BAND), F32),
            lags((2, bands)), lags((bands, 2)), lags((blocks - 1, bands)), lags((bands, 2)),
            pltpu.VMEM((bands, 2, kept, BAND), F32),
            pltpu.VMEM((2 * (REACH + 1), BAND), F32),
            dma((pieces,)), dma((pieces,)), dma((pieces,)), dma((pieces,)),
            dma((2, bands)), dma((blocks - 1, bands)),
            dma((bands,)), dma((bands,)), dma((bands,)), dma((bands,)),
            dma((blocks - 1,)), dma((1,)),
            dma((groups,)), dma((1,)), dma((1,)),
        ],
        compiler_params=pltpu.CompilerParams(
            collective_id=0, has_side_effects=True, vmem_limit_bytes=60 * 1024 * 1024
        ),
    )(spectra, counts, owners, forward, inverse)
    return out[:, None]


def solution(mesh):
    sizes = dict(mesh.shape)
    fits = sizes["cable"] == REACH + 1 and sizes["pairs"] == 2
    shards = four_block_shards if fits else general_shards
    placed = (
        P("groups", None, "cable", "bins"),
        P(("groups", "cable")),
        P(("groups", "cable"), None),
    )
    return jax.shard_map(
        shards,
        mesh=mesh,
        in_specs=placed,
        out_specs=P("groups", "cable", "pairs", "bins"),
        check_vma=False,
    )
```

```python
import math

import jax
import jax.numpy as jnp
import numpy as np
from jax import lax
from jax.experimental import pallas as pl
from jax.experimental.pallas import tpu as pltpu
from jax.sharding import PartitionSpec as P

REACH = 3
HALF_WIDTH = 32


epsilon = 1e-06
band_rows = 16


def with_halo(x, sides, width):
    for axis, dim in sides:
        count, length = (lax.axis_size(axis), x.shape[dim])
        up = [(i, (i + 1) % count) for i in range(count - 1)]
        down = [(j, i) for i, j in up]
        last = lax.slice_in_dim(x, length - width, length, axis=dim)
        first = lax.slice_in_dim(x, 0, width, axis=dim)
        before = lax.ppermute(last, axis, up)
        after = lax.ppermute(first, axis, down)
        x = jnp.concatenate([before, x, after], axis=dim)
    return x


def from_behind(block, axis, distance):
    devices = range(lax.axis_size(axis))
    route = [(i - distance, i) for i in devices if i - distance in devices]
    return lax.ppermute(block, axis, route)


def whiten_rows(spectra):
    real_part = spectra[0].astype(jnp.float32)
    imag_part = spectra[1].astype(jnp.float32)
    power_sum = real_part * real_part + imag_part * imag_part
    padded = with_halo(power_sum, (("bins", 2),), HALF_WIDTH)
    window_len = 2 * HALF_WIDTH + 1
    window_sum = lax.reduce_window(
        padded, jnp.zeros((), padded.dtype), lax.add, (1, 1, window_len), (1, 1, 1), "VALID"
    )
    inverse_amp = lax.rsqrt(window_sum / window_len + epsilon)
    return jnp.stack(
        [
            (real_part * inverse_amp).astype(jnp.bfloat16),
            (imag_part * inverse_amp).astype(jnp.bfloat16),
        ]
    )


def make_lag_table(col_count):
    flattened = jnp.arange(band_rows * col_count)
    row_of = flattened // col_count
    col_of = flattened % col_count
    lag_lanes = jnp.arange(col_count + band_rows - 1)
    return (lag_lanes[None, :] == (col_of - row_of + band_rows - 1)[:, None]).astype(jnp.bfloat16)


def lag_stack(pair_block, lag_table):
    freq_count, row_count, col_count = pair_block.shape
    group_count = row_count // band_rows
    grouped = pair_block.reshape(freq_count, group_count, band_rows * col_count)
    banded = jnp.einsum("fgk,ku->fgu", grouped, lag_table, preferred_element_type=jnp.float32)
    lag_sums = jnp.zeros((freq_count, col_count + row_count - 1), jnp.float32)
    for row_group in range(group_count):
        first_lag = row_count - band_rows * (row_group + 1)
        lag_sums = lag_sums.at[:, first_lag : first_lag + col_count + band_rows - 1].add(
            banded[:, row_group]
        )
    return lag_sums.T


def correlate(left_rows, right_rows, factor, lag_table):
    left_real = jnp.concatenate([left_rows[0], left_rows[1]], axis=0)
    left_imag = jnp.concatenate([left_rows[1], -left_rows[0]], axis=0)
    right_both = jnp.concatenate([right_rows[0], right_rows[1]], axis=0)
    corr_real = (
        jnp.einsum("wif,wjf->fij", left_real, right_both, preferred_element_type=jnp.float32)
        * factor
    ).astype(jnp.bfloat16)
    corr_imag = (
        jnp.einsum("wif,wjf->fij", left_imag, right_both, preferred_element_type=jnp.float32)
        * factor
    ).astype(jnp.bfloat16)
    return jnp.stack([lag_stack(corr_real, lag_table), lag_stack(corr_imag, lag_table)])


def general_shards(spectra, counts, owners):
    pair_devs = lax.axis_size("pairs")
    member = lax.axis_index("pairs")
    channels = spectra.shape[2]
    half_rows = channels // pair_devs
    source = whiten_rows(spectra)
    receiver = lax.dynamic_slice_in_dim(source, member * half_rows, half_rows, 2)
    block_count = lax.axis_size("cable")
    cable_index = lax.axis_index("cable")
    live_count = jnp.minimum(counts[0], block_count - cable_index)
    panels = {0: receiver}
    for offset in range(1, REACH + 1):
        panels[offset] = from_behind(receiver, "cable", -offset)
    factor = 1.0 / math.sqrt(source.shape[1] * channels)
    lag_table = make_lag_table(half_rows)
    freq_count = source.shape[3]
    stacks = jnp.zeros((2, (REACH + 2) * channels, freq_count), jnp.float32)
    for offset in range(REACH + 1):
        lag_piece = correlate(source, panels[offset], factor, lag_table)
        weight = (offset < live_count).astype(jnp.float32)
        if offset == 0:
            kept_here = weight * lag_piece
        else:
            sent_away = owners[0, offset].astype(jnp.float32)
            arrived = from_behind(weight * sent_away * lag_piece, "cable", offset)
            kept_here = weight * (1.0 - sent_away) * lag_piece + arrived
        first_lag = offset * channels + member * half_rows
        current = lax.dynamic_slice_in_dim(stacks, first_lag, kept_here.shape[1], 1)
        stacks = lax.dynamic_update_slice_in_dim(stacks, current + kept_here, first_lag, 1)
    summed = lax.psum_scatter(stacks, "pairs", scatter_dimension=1, tiled=True)
    return summed[:, None]


EDGE = 128
BAND = 128
GROUP = 2
EARLY = 3
F32 = jnp.float32
MESH = pl.DeviceIdType.MESH


def channel_transforms(channels, factor):
    points = 2 * channels
    index = np.arange(points)
    angle = 2 * np.pi * np.outer(index, np.arange(channels)) / points
    cos, sin = np.cos(angle), np.sin(angle)
    full = np.block([[cos, sin], [-sin, cos]])
    high = full.astype(jnp.bfloat16)
    low = (full - high.astype(np.float64)).astype(jnp.bfloat16)
    forward = np.concatenate([high, low], axis=1)
    angle = 2 * np.pi * np.outer(index - (channels - 1), index) / points
    cos, sin = np.cos(angle), np.sin(angle)
    cos[-1], sin[-1] = 0.0, 0.0
    inverse = np.block([[cos, sin], [-sin, cos]]) * (factor / points)
    return jnp.asarray(forward), jnp.asarray(inverse.astype(np.float32))


def smoothing_window():
    distance = np.arange(BAND + 2 * EDGE)[:, None] - (np.arange(BAND)[None, :] + EDGE)
    ones = (np.abs(distance) <= HALF_WIDTH).astype(jnp.bfloat16)
    return jnp.asarray(np.concatenate([ones, ones], axis=0))


def stack_kernel(
    spectra_ref, counts_ref, owners_ref, window_ref, forward_ref, inverse_ref, out_ref,
    x_ref, flag_ref, white, far, back, spec, other, third, sums, sums_back, sums_far, stack, piece_out, piece_back, piece_in, arrived, swapped, seen,
    chain_send, chain_recv, back_send, back_recv, piece_send, piece_recv,
    next_send, next_recv, swap_send, swap_recv, flag_send, flag_recv, load_sem, edge_send, edge_recv,
):
    windows, channels = x_ref.shape[1:3]
    half = x_ref.shape[3] - 2 * EDGE
    bands, groups = half // BAND, windows // GROUP
    points = 2 * channels
    kept = out_ref.shape[1]
    blocks, halves = lax.axis_size("cable"), lax.axis_size("pairs")
    z, m = lax.axis_index("cable"), lax.axis_index("pairs")
    cuts, x = lax.axis_size("bins"), lax.axis_index("bins")
    bins = spectra_ref.shape[3]
    first = m == 0
    mirrored = jnp.where((x > 0) & (first | (x == cuts - 1)), 1, 0)
    onward = {"cable": lax.rem(z + 1, blocks)}
    backward = {"cable": lax.rem(z + blocks - 1, blocks)}
    partner = {"pairs": lax.rem(m + 1, halves)}

    def remote(source, target, send, recv, device):
        return pltpu.make_async_remote_copy(
            src_ref=source, dst_ref=target, send_sem=send, recv_sem=recv, device_id=device, device_id_type=MESH
        )

    def first_hop(s):
        return remote(white.at[s], far.at[s], chain_send.at[s], chain_recv.at[s], onward)

    def next_hop(s):
        return remote(far.at[s], far.at[s], chain_send.at[s], chain_recv.at[s], onward)

    def back_hop(s):
        return remote(white.at[s], back.at[s], back_send.at[s], back_recv.at[s], backward)

    def to_first(c, kind, slot):
        return remote(
            piece_out.at[kind, c], piece_in.at[slot, c], piece_send.at[kind, c], piece_recv.at[slot, c], {"cable": 0}
        )

    def to_next(c):
        return remote(piece_back.at[c], arrived.at[c], next_send.at[c], next_recv.at[c], onward)

    def swap(c):
        rows = pl.ds(pl.multiple_of((1 - m) * kept, 8), kept)
        return remote(
            stack.at[c, :, rows], swapped.at[place(c)], swap_send.at[c], swap_recv.at[place(c)], partner
        )

    def place(c):
        return c + mirrored * (bands - 1 - 2 * c)

    def load(q):
        near = pl.multiple_of(m * (half - EDGE), EDGE)
        spot = pl.multiple_of((1 - m) * EDGE, EDGE)
        rows = pl.ds(q * GROUP, GROUP)
        return pltpu.make_async_copy(
            spectra_ref.at[:, rows, :, pl.ds(near, half + EDGE)],
            x_ref.at[:, rows, :, pl.ds(spot, half + EDGE)],
            load_sem.at[q],
        )

    spot = pl.ds(pl.multiple_of(m * (half + EDGE), EDGE), EDGE)

    def edge():
        source = pl.ds(pl.multiple_of((1 - m) * (bins - EDGE), EDGE), EDGE)
        target = {"bins": lax.rem(x + cuts + 1 - 2 * m, cuts)}
        return remote(
            spectra_ref.at[:, :, :, source], x_ref.at[:, :, :, spot], edge_send.at[0], edge_recv.at[0], target
        )

    def flags_to(block):
        return remote(flag_ref, seen, flag_send.at[block - 1], flag_recv.at[0], {"cable": block})

    for q in range(groups):
        load(q).start()
    live = jnp.minimum(counts_ref[0], blocks - z)
    for offset in range(REACH + 1):
        flag_ref[offset : offset + 1, :] = jnp.full((1, BAND), owners_ref[0, offset].astype(F32))
        weight = jnp.where(offset < live, 1.0, 0.0)
        flag_ref[REACH + 1 + offset : REACH + 2 + offset, :] = jnp.full((1, BAND), weight)
    barrier = pltpu.get_barrier_semaphore()
    for step in range(1, blocks):
        pl.semaphore_signal(barrier, inc=1, device_id={"cable": lax.rem(z + step, blocks)}, device_id_type=MESH)
    pl.semaphore_signal(barrier, inc=1, device_id=partner, device_id_type=MESH)
    for step in range(1, cuts):
        pl.semaphore_signal(barrier, inc=1, device_id={"bins": lax.rem(x + step, cuts)}, device_id_type=MESH)
    pl.semaphore_wait(barrier, blocks + cuts - 1)
    sends_edge = (first & (x < cuts - 1)) | (~first & (x > 0))
    takes_edge = (first & (x > 0)) | (~first & (x < cuts - 1))

    @pl.when(sends_edge)
    def _():
        edge().start()

    @pl.when(~takes_edge)
    def _():
        x_ref[:, :, :, spot] = jnp.zeros((2, windows, channels, EDGE), x_ref.dtype)


    @pl.when(z == 0)
    def _():
        for block in range(1, blocks - 1):
            flags_to(block).start()

    def whiten(q, begin, count, store):
        lanes = pl.ds(pl.multiple_of(begin, BAND), count * BAND + 2 * EDGE)
        reals, imags, highs, lows = [], [], [], []
        for i in range(GROUP):
            real = x_ref[0, q * GROUP + i, :, lanes].astype(F32)
            imag = x_ref[1, q * GROUP + i, :, lanes].astype(F32)
            power = real * real + imag * imag
            high = power.astype(jnp.bfloat16)
            reals.append(real)
            imags.append(imag)
            highs.append(high)
            lows.append((power - high.astype(F32)).astype(jnp.bfloat16))
        high = jnp.concatenate(highs, axis=0)
        low = jnp.concatenate(lows, axis=0)
        for j in range(count):
            reach = slice(j * BAND, (j + 1) * BAND + 2 * EDGE)
            terms = jnp.concatenate([high[:, reach], low[:, reach]], axis=1)
            total = jnp.dot(terms, window_ref[...], preferred_element_type=F32)
            gain = lax.rsqrt(total / (2 * HALF_WIDTH + 1) + epsilon)
            here = slice(EDGE + j * BAND, EDGE + (j + 1) * BAND)
            slot = store(j) * groups + q
            for i in range(GROUP):
                rows = gain[i * channels : (i + 1) * channels]
                white[slot, i, :channels] = (reals[i][:, here] * rows).astype(jnp.bfloat16)
                white[slot, i, channels:] = (imags[i][:, here] * rows).astype(jnp.bfloat16)

    def whiten_inner(q, carry):
        load(q).wait()
        whiten(q, mirrored * BAND, bands - 1, lambda j: j + mirrored * (bands - 2 - 2 * j))

        @pl.when(z == 0)
        def _():
            first_hop(q).start()

        @pl.when(z == blocks - 1)
        def _():
            back_hop(q).start()

        return carry

    def whiten_last(q, carry):
        whiten(q, (1 - mirrored) * (bands - 1) * BAND, 1, lambda j: bands - 1)
        s = (bands - 1) * groups + q

        @pl.when(z == 0)
        def _():
            first_hop(s).start()

        @pl.when(z == blocks - 1)
        def _():
            back_hop(s).start()

        return carry

    def relay(s):
        next_hop(s).wait_recv()
        next_hop(s).start()

    def relay_early(s, count):
        @pl.when(z == 1)
        def _():
            for k in range(count):
                relay(s + k)

    lax.fori_loop(0, groups, whiten_inner, 0)
    relay_early(0, 1)

    @pl.when(z == 0)
    def _():
        @pl.loop(groups, (bands - 1) * groups)
        def _(s):
            first_hop(s).start()

    @pl.when(z == blocks - 1)
    def _():
        @pl.loop(groups, (bands - 1) * groups)
        def _(s):
            back_hop(s).start()

    @pl.when(takes_edge)
    def _():
        edge().wait_recv()

    lax.fori_loop(0, groups, whiten_last, 0)
    relay_early(1, 2)

    def transform(buffer, s):
        wide = jnp.concatenate([buffer[s, i] for i in range(GROUP)], axis=1)
        return jnp.dot(forward_ref[...], jnp.concatenate([wide, wide], axis=0), preferred_element_type=F32)

    tile = 32

    def power_into(total, s):
        for k in range(0, points, tile):
            gained = total[k : k + tile]
            for i in range(GROUP):
                lanes = slice(i * BAND, (i + 1) * BAND)
                real = spec[s, k : k + tile, lanes]
                imag = spec[s, points + k : points + k + tile, lanes]
                gained = gained + (real * real + imag * imag)
            total[k : k + tile] = gained

    def cross_into(total, near, far):
        for k in range(0, points, tile):
            gained_real = total[k : k + tile]
            gained_imag = total[points + k : points + k + tile]
            for i in range(GROUP):
                lanes = slice(i * BAND, (i + 1) * BAND)
                near_real = near[k : k + tile, lanes]
                near_imag = near[points + k : points + k + tile, lanes]
                far_real = far[k : k + tile, lanes]
                far_imag = far[points + k : points + k + tile, lanes]
                gained_real = gained_real + (near_real * far_real + near_imag * far_imag)
                gained_imag = gained_imag + (near_imag * far_real - near_real * far_imag)
            total[k : k + tile] = gained_real
            total[points + k : points + k + tile] = gained_imag

    def lags_of(values, columns):
        return jnp.dot(
            inverse_ref[:, :columns], values, preferred_element_type=F32, precision=lax.Precision.HIGHEST
        )

    def add_piece(c, first, piece):
        rows = pl.ds(first, points)
        stack[c, 0, rows] += piece[:points]
        stack[c, 1, rows] += piece[points:]

    def own_band(c, carry):
        sums[...] = jnp.zeros_like(sums)

        def step(q, inner):
            s = c * groups + q
            spec[s] = transform(white, s)
            power_into(sums, s)
            return inner

        lax.fori_loop(0, groups, step, 0)
        stack[c] = jnp.zeros(stack.shape[1:], F32)
        add_piece(c, 0, flag_ref[REACH + 1 : REACH + 2, :] * lags_of(sums[:points], points))
        relay_early(EARLY + c, 1)
        return carry

    lax.fori_loop(0, bands, own_band, 0)

    def counted_far(offset):
        return seen[offset : offset + 1, :] * seen[REACH + 1 + offset : REACH + 2 + offset, :]

    @pl.when(z == 1)
    def _():
        flags_to(1).wait_recv()

        def band(c, carry):
            sums[...] = jnp.zeros_like(sums)

            def step(q, inner):
                s = c * groups + q

                @pl.when(s >= EARLY + bands)
                def _():
                    relay(s)

                other[...] = transform(far, s)
                cross_into(sums, other, spec.at[s])
                return inner

            lax.fori_loop(0, groups, step, 0)
            piece = lags_of(sums[...], 2 * points)
            piece_out[0, c] = piece.astype(piece_out.dtype)
            to_first(c, 0, 0).start()
            add_piece(c, channels, counted_far(1) * piece)
            swap(c).start()
            return carry

        lax.fori_loop(0, bands, band, 0)

    @pl.when(z == 2)
    def _():
        flags_to(1).wait_recv()

        def band(c, carry):
            sums[...] = jnp.zeros_like(sums)
            sums_back[...] = jnp.zeros_like(sums_back)
            sums_far[...] = jnp.zeros_like(sums_far)

            def step(q, inner):
                s = c * groups + q
                back_hop(s).wait_recv()
                third[...] = transform(back, s)
                cross_into(sums_back, spec.at[s], third)
                next_hop(s).wait_recv()
                other[...] = transform(far, s)
                cross_into(sums, other, spec.at[s])
                cross_into(sums_far, other, third)
                return inner

            lax.fori_loop(0, groups, step, 0)
            piece = lags_of(sums[...], 2 * points)
            piece_out[0, c] = piece.astype(piece_out.dtype)
            to_first(c, 0, 1).start()
            distant = lags_of(sums_far[...], 2 * points)
            piece_out[1, c] = distant.astype(piece_out.dtype)
            to_first(c, 1, 2).start()
            ahead = flag_ref[REACH + 2 : REACH + 3, :] * lags_of(sums_back[...], 2 * points)
            sent = flag_ref[1:2, :]
            piece_back[c, 0] = (sent * ahead).astype(piece_back.dtype)
            piece_back[c, 1] = (counted_far(3) * distant).astype(piece_back.dtype)
            to_next(c).start()
            add_piece(c, 2 * channels, counted_far(2) * piece)
            add_piece(c, channels, (1.0 - sent) * ahead)
            swap(c).start()
            return carry

        lax.fori_loop(0, bands, band, 0)

    @pl.when(z == blocks - 1)
    def _():
        def band(c, carry):
            to_next(c).wait_recv()
            add_piece(c, channels, arrived[c, 0].astype(F32))
            add_piece(c, 3 * channels, arrived[c, 1].astype(F32))
            swap(c).start()
            return carry

        lax.fori_loop(0, bands, band, 0)

    @pl.when(z == 0)
    def _():
        def band(c, carry):
            for offset in range(1, blocks):
                to_first(c, 0, offset - 1).wait_recv()
                counted = (1.0 - flag_ref[offset : offset + 1, :]) * flag_ref[REACH + 1 + offset : REACH + 2 + offset, :]
                add_piece(c, offset * channels, counted * piece_in[offset - 1, c].astype(F32))
            swap(c).start()
            return carry

        lax.fori_loop(0, bands, band, 0)

    def collect(c, carry):
        mine = pl.ds(pl.multiple_of(m * half + place(c) * BAND, BAND), BAND)
        theirs = pl.ds(pl.multiple_of((1 - m) * half + place(c) * BAND, BAND), BAND)
        out_ref[:, :, mine] = stack[c, :, pl.ds(pl.multiple_of(m * kept, 8), kept)]
        swap(c).wait_recv()
        out_ref[:, :, theirs] = swapped[place(c)]
        swap(c).wait_send()
        return carry

    lax.fori_loop(0, bands, collect, 0)

    @pl.when(sends_edge)
    def _():
        edge().wait_send()

    @pl.when(z < 2)
    def _():
        @pl.loop(0, bands * groups)
        def _(s):
            next_hop(s).wait_send()

    @pl.when(z == blocks - 1)
    def _():
        @pl.loop(0, bands * groups)
        def _(s):
            back_hop(s).wait_send()

    @pl.when((z == 1) | (z == 2))
    def _():
        @pl.loop(0, bands)
        def _(c):
            to_first(c, 0, z - 1).wait_send()

    @pl.when(z == 2)
    def _():
        @pl.loop(0, bands)
        def _(c):
            to_first(c, 1, 2).wait_send()
            to_next(c).wait_send()

    @pl.when(z == 0)
    def _():
        for block in range(1, blocks - 1):
            flags_to(block).wait_send()


def four_block_shards(spectra, counts, owners):
    parts, windows, channels, bins = spectra.shape
    halves, blocks = lax.axis_size("pairs"), lax.axis_size("cable")
    half, points = bins // halves, 2 * channels
    forward, inverse = channel_transforms(channels, 1.0 / math.sqrt(windows * channels))
    bands, groups = half // BAND, windows // GROUP
    pieces = bands * groups
    rows = (REACH + 2) * channels
    kept = rows // halves
    block = pltpu.VMEM((pieces, GROUP, points, BAND), jnp.bfloat16)
    spectrum = pltpu.VMEM((2 * points, GROUP * BAND), F32)
    sums = pltpu.VMEM((2 * points, BAND), F32)

    def lags(lead):
        return pltpu.VMEM(lead + (2 * points, BAND), jnp.bfloat16)

    dma = pltpu.SemaphoreType.DMA
    out = pl.pallas_call(
        stack_kernel,
        out_shape=jax.ShapeDtypeStruct((2, kept, bins), F32),
        in_specs=[
            pl.BlockSpec(memory_space=pl.ANY),
            pl.BlockSpec(memory_space=pltpu.SMEM),
            pl.BlockSpec(memory_space=pltpu.SMEM),
            pl.BlockSpec(memory_space=pltpu.VMEM),
            pl.BlockSpec(memory_space=pltpu.VMEM),
            pl.BlockSpec(memory_space=pltpu.VMEM),
        ],
        out_specs=pl.BlockSpec(memory_space=pltpu.VMEM),
        scratch_shapes=[
            pltpu.VMEM((2, windows, channels, half + 2 * EDGE), jnp.bfloat16),
            pltpu.VMEM((2 * (REACH + 1), BAND), F32),
            block, block, block,
            pltpu.VMEM((pieces, 2 * points, GROUP * BAND), F32),
            spectrum, spectrum, sums, sums, sums,
            pltpu.VMEM((bands, 2, rows, BAND), F32),
            lags((2, bands)), lags((bands, 2)), lags((blocks - 1, bands)), lags((bands, 2)),
            pltpu.VMEM((bands, 2, kept, BAND), F32),
            pltpu.VMEM((2 * (REACH + 1), BAND), F32),
            dma((pieces,)), dma((pieces,)), dma((pieces,)), dma((pieces,)),
            dma((2, bands)), dma((blocks - 1, bands)),
            dma((bands,)), dma((bands,)), dma((bands,)), dma((bands,)),
            dma((blocks - 1,)), dma((1,)),
            dma((groups,)), dma((1,)), dma((1,)),
        ],
        compiler_params=pltpu.CompilerParams(
            collective_id=0, has_side_effects=True, vmem_limit_bytes=60 * 1024 * 1024
        ),
    )(spectra, counts, owners, smoothing_window(), forward, inverse)
    return out[:, None]


def solution(mesh):
    sizes = dict(mesh.shape)
    fits = sizes["cable"] == REACH + 1 and sizes["pairs"] == 2
    shards = four_block_shards if fits else general_shards
    placed = (
        P("groups", None, "cable", "bins"),
        P(("groups", "cable")),
        P(("groups", "cable"), None),
    )
    return jax.shard_map(
        shards,
        mesh=mesh,
        in_specs=placed,
        out_specs=P("groups", "cable", "pairs", "bins"),
        check_vma=False,
    )
```

```python
import math

import jax
import jax.numpy as jnp
import numpy as np
from jax import lax
from jax.experimental import pallas as pl
from jax.experimental.pallas import tpu as pltpu
from jax.sharding import PartitionSpec as P

REACH = 3
HALF_WIDTH = 32


epsilon = 1e-06
band_rows = 16


def with_halo(x, sides, width):
    for axis, dim in sides:
        count, length = (lax.axis_size(axis), x.shape[dim])
        up = [(i, (i + 1) % count) for i in range(count - 1)]
        down = [(j, i) for i, j in up]
        last = lax.slice_in_dim(x, length - width, length, axis=dim)
        first = lax.slice_in_dim(x, 0, width, axis=dim)
        before = lax.ppermute(last, axis, up)
        after = lax.ppermute(first, axis, down)
        x = jnp.concatenate([before, x, after], axis=dim)
    return x


def from_behind(block, axis, distance):
    devices = range(lax.axis_size(axis))
    route = [(i - distance, i) for i in devices if i - distance in devices]
    return lax.ppermute(block, axis, route)


def whiten_rows(spectra):
    real_part = spectra[0].astype(jnp.float32)
    imag_part = spectra[1].astype(jnp.float32)
    power_sum = real_part * real_part + imag_part * imag_part
    padded = with_halo(power_sum, (("bins", 2),), HALF_WIDTH)
    window_len = 2 * HALF_WIDTH + 1
    window_sum = lax.reduce_window(
        padded, jnp.zeros((), padded.dtype), lax.add, (1, 1, window_len), (1, 1, 1), "VALID"
    )
    inverse_amp = lax.rsqrt(window_sum / window_len + epsilon)
    return jnp.stack(
        [
            (real_part * inverse_amp).astype(jnp.bfloat16),
            (imag_part * inverse_amp).astype(jnp.bfloat16),
        ]
    )


def make_lag_table(col_count):
    flattened = jnp.arange(band_rows * col_count)
    row_of = flattened // col_count
    col_of = flattened % col_count
    lag_lanes = jnp.arange(col_count + band_rows - 1)
    return (lag_lanes[None, :] == (col_of - row_of + band_rows - 1)[:, None]).astype(jnp.bfloat16)


def lag_stack(pair_block, lag_table):
    freq_count, row_count, col_count = pair_block.shape
    group_count = row_count // band_rows
    grouped = pair_block.reshape(freq_count, group_count, band_rows * col_count)
    banded = jnp.einsum("fgk,ku->fgu", grouped, lag_table, preferred_element_type=jnp.float32)
    lag_sums = jnp.zeros((freq_count, col_count + row_count - 1), jnp.float32)
    for row_group in range(group_count):
        first_lag = row_count - band_rows * (row_group + 1)
        lag_sums = lag_sums.at[:, first_lag : first_lag + col_count + band_rows - 1].add(
            banded[:, row_group]
        )
    return lag_sums.T


def correlate(left_rows, right_rows, factor, lag_table):
    left_real = jnp.concatenate([left_rows[0], left_rows[1]], axis=0)
    left_imag = jnp.concatenate([left_rows[1], -left_rows[0]], axis=0)
    right_both = jnp.concatenate([right_rows[0], right_rows[1]], axis=0)
    corr_real = (
        jnp.einsum("wif,wjf->fij", left_real, right_both, preferred_element_type=jnp.float32)
        * factor
    ).astype(jnp.bfloat16)
    corr_imag = (
        jnp.einsum("wif,wjf->fij", left_imag, right_both, preferred_element_type=jnp.float32)
        * factor
    ).astype(jnp.bfloat16)
    return jnp.stack([lag_stack(corr_real, lag_table), lag_stack(corr_imag, lag_table)])


def general_shards(spectra, counts, owners):
    pair_devs = lax.axis_size("pairs")
    member = lax.axis_index("pairs")
    channels = spectra.shape[2]
    half_rows = channels // pair_devs
    source = whiten_rows(spectra)
    receiver = lax.dynamic_slice_in_dim(source, member * half_rows, half_rows, 2)
    block_count = lax.axis_size("cable")
    cable_index = lax.axis_index("cable")
    live_count = jnp.minimum(counts[0], block_count - cable_index)
    panels = {0: receiver}
    for offset in range(1, REACH + 1):
        panels[offset] = from_behind(receiver, "cable", -offset)
    factor = 1.0 / math.sqrt(source.shape[1] * channels)
    lag_table = make_lag_table(half_rows)
    freq_count = source.shape[3]
    stacks = jnp.zeros((2, (REACH + 2) * channels, freq_count), jnp.float32)
    for offset in range(REACH + 1):
        lag_piece = correlate(source, panels[offset], factor, lag_table)
        weight = (offset < live_count).astype(jnp.float32)
        if offset == 0:
            kept_here = weight * lag_piece
        else:
            sent_away = owners[0, offset].astype(jnp.float32)
            arrived = from_behind(weight * sent_away * lag_piece, "cable", offset)
            kept_here = weight * (1.0 - sent_away) * lag_piece + arrived
        first_lag = offset * channels + member * half_rows
        current = lax.dynamic_slice_in_dim(stacks, first_lag, kept_here.shape[1], 1)
        stacks = lax.dynamic_update_slice_in_dim(stacks, current + kept_here, first_lag, 1)
    summed = lax.psum_scatter(stacks, "pairs", scatter_dimension=1, tiled=True)
    return summed[:, None]


EDGE = 128
BAND = 128
GROUP = 2
EARLY = 3
F32 = jnp.float32
MESH = pl.DeviceIdType.MESH


def channel_transforms(channels, factor):
    points = 2 * channels
    index = np.arange(points)
    angle = 2 * np.pi * np.outer(index, np.arange(channels)) / points
    cos, sin = np.cos(angle), np.sin(angle)
    full = np.block([[cos, sin], [-sin, cos]])
    high = full.astype(jnp.bfloat16)
    low = (full - high.astype(np.float64)).astype(jnp.bfloat16)
    forward = np.concatenate([high, low], axis=1)
    angle = 2 * np.pi * np.outer(index - (channels - 1), index) / points
    cos, sin = np.cos(angle), np.sin(angle)
    cos[-1], sin[-1] = 0.0, 0.0
    inverse = np.block([[cos, sin], [-sin, cos]]) * (factor / points)
    return jnp.asarray(forward), jnp.asarray(inverse.astype(np.float32))


def smoothing_window():
    distance = np.arange(BAND + 2 * EDGE)[:, None] - (np.arange(BAND)[None, :] + EDGE)
    ones = (np.abs(distance) <= HALF_WIDTH).astype(jnp.bfloat16)
    return jnp.asarray(np.concatenate([ones, ones], axis=0))


def stack_kernel(
    spectra_ref, counts_ref, owners_ref, window_ref, forward_ref, inverse_ref, out_ref,
    x_ref, flag_ref, white, far, back, spec, other, third, sums, sums_back, sums_far, stack, near_out, piece_back, near_in, arrived, swapped, seen,
    chain_send, chain_recv, back_send, back_recv, piece_send, piece_recv,
    next_send, next_recv, swap_send, swap_recv, flag_send, flag_recv, load_sem, edge_send, edge_recv,
):
    windows, channels = x_ref.shape[1:3]
    half = x_ref.shape[3] - 2 * EDGE
    bands, groups = half // BAND, windows // GROUP
    points = 2 * channels
    kept = out_ref.shape[1]
    blocks, halves = lax.axis_size("cable"), lax.axis_size("pairs")
    z, m = lax.axis_index("cable"), lax.axis_index("pairs")
    cuts, x = lax.axis_size("bins"), lax.axis_index("bins")
    bins = spectra_ref.shape[3]
    first = m == 0
    mirrored = jnp.where((x > 0) & (first | (x == cuts - 1)), 1, 0)
    onward = {"cable": lax.rem(z + 1, blocks)}
    backward = {"cable": lax.rem(z + blocks - 1, blocks)}
    partner = {"pairs": lax.rem(m + 1, halves)}

    def remote(source, target, send, recv, device):
        return pltpu.make_async_remote_copy(
            src_ref=source, dst_ref=target, send_sem=send, recv_sem=recv, device_id=device, device_id_type=MESH
        )

    def first_hop(s):
        return remote(white.at[s], far.at[s], chain_send.at[s], chain_recv.at[s], onward)

    def next_hop(s):
        return remote(far.at[s], far.at[s], chain_send.at[s], chain_recv.at[s], onward)

    def back_hop(s):
        return remote(white.at[s], back.at[s], back_send.at[s], back_recv.at[s], backward)

    def near_rows(source, target):
        begin, end = source * channels, source * channels + points + (source - 1) * channels
        return begin, max(begin, target * kept), min(end, (target + 1) * kept)

    def to_first(c, source, target, sender, spot_of):
        begin, low, high = near_rows(source, target)
        return remote(
            near_out.at[c, :, low - begin : high - begin],
            near_in.at[source - 1, sender, spot_of, :, low - target * kept : high - target * kept],
            piece_send.at[target, c],
            piece_recv.at[source - 1, sender, spot_of],
            {"cable": 0, "pairs": target},
        )

    def to_next(c):
        return remote(piece_back.at[c], arrived.at[c], next_send.at[c], next_recv.at[c], onward)

    def swap(c):
        rows = pl.ds(pl.multiple_of((1 - m) * kept, 8), kept)
        return remote(
            stack.at[c, :, rows], swapped.at[place(c)], swap_send.at[c], swap_recv.at[place(c)], partner
        )

    def place(c):
        return c + mirrored * (bands - 1 - 2 * c)

    def load(q):
        near = pl.multiple_of(m * (half - EDGE), EDGE)
        spot = pl.multiple_of((1 - m) * EDGE, EDGE)
        rows = pl.ds(q * GROUP, GROUP)
        return pltpu.make_async_copy(
            spectra_ref.at[:, rows, :, pl.ds(near, half + EDGE)],
            x_ref.at[:, rows, :, pl.ds(spot, half + EDGE)],
            load_sem.at[q],
        )

    spot = pl.ds(pl.multiple_of(m * (half + EDGE), EDGE), EDGE)

    def edge():
        source = pl.ds(pl.multiple_of((1 - m) * (bins - EDGE), EDGE), EDGE)
        target = {"bins": lax.rem(x + cuts + 1 - 2 * m, cuts)}
        return remote(
            spectra_ref.at[:, :, :, source], x_ref.at[:, :, :, spot], edge_send.at[0], edge_recv.at[0], target
        )

    def flags_to(block):
        return remote(flag_ref, seen, flag_send.at[block - 1], flag_recv.at[0], {"cable": block})

    for q in range(groups):
        load(q).start()
    live = jnp.minimum(counts_ref[0], blocks - z)
    for offset in range(REACH + 1):
        flag_ref[offset : offset + 1, :] = jnp.full((1, BAND), owners_ref[0, offset].astype(F32))
        weight = jnp.where(offset < live, 1.0, 0.0)
        flag_ref[REACH + 1 + offset : REACH + 2 + offset, :] = jnp.full((1, BAND), weight)
    barrier = pltpu.get_barrier_semaphore()
    for step in range(1, blocks):
        pl.semaphore_signal(barrier, inc=1, device_id={"cable": lax.rem(z + step, blocks)}, device_id_type=MESH)
        across = {"cable": lax.rem(z + step, blocks), "pairs": lax.rem(m + 1, halves)}
        pl.semaphore_signal(barrier, inc=1, device_id=across, device_id_type=MESH)
    pl.semaphore_signal(barrier, inc=1, device_id=partner, device_id_type=MESH)
    for step in range(1, cuts):
        pl.semaphore_signal(barrier, inc=1, device_id={"bins": lax.rem(x + step, cuts)}, device_id_type=MESH)
    pl.semaphore_wait(barrier, 2 * blocks + cuts - 2)
    sends_edge = (first & (x < cuts - 1)) | (~first & (x > 0))
    takes_edge = (first & (x > 0)) | (~first & (x < cuts - 1))

    @pl.when(sends_edge)
    def _():
        edge().start()

    @pl.when(~takes_edge)
    def _():
        x_ref[:, :, :, spot] = jnp.zeros((2, windows, channels, EDGE), x_ref.dtype)


    @pl.when(z == 0)
    def _():
        for block in range(1, blocks - 1):
            flags_to(block).start()

    def whiten(q, begin, count, store):
        lanes = pl.ds(pl.multiple_of(begin, BAND), count * BAND + 2 * EDGE)
        reals, imags, highs, lows = [], [], [], []
        for i in range(GROUP):
            real = x_ref[0, q * GROUP + i, :, lanes].astype(F32)
            imag = x_ref[1, q * GROUP + i, :, lanes].astype(F32)
            power = real * real + imag * imag
            high = power.astype(jnp.bfloat16)
            reals.append(real)
            imags.append(imag)
            highs.append(high)
            lows.append((power - high.astype(F32)).astype(jnp.bfloat16))
        high = jnp.concatenate(highs, axis=0)
        low = jnp.concatenate(lows, axis=0)
        for j in range(count):
            reach = slice(j * BAND, (j + 1) * BAND + 2 * EDGE)
            terms = jnp.concatenate([high[:, reach], low[:, reach]], axis=1)
            total = jnp.dot(terms, window_ref[...], preferred_element_type=F32)
            gain = lax.rsqrt(total / (2 * HALF_WIDTH + 1) + epsilon)
            here = slice(EDGE + j * BAND, EDGE + (j + 1) * BAND)
            slot = store(j) * groups + q
            for i in range(GROUP):
                rows = gain[i * channels : (i + 1) * channels]
                white[slot, i, :channels] = (reals[i][:, here] * rows).astype(jnp.bfloat16)
                white[slot, i, channels:] = (imags[i][:, here] * rows).astype(jnp.bfloat16)

    def whiten_inner(q, carry):
        load(q).wait()
        whiten(q, mirrored * BAND, bands - 1, lambda j: j + mirrored * (bands - 2 - 2 * j))

        @pl.when(z == 0)
        def _():
            first_hop(q).start()

        @pl.when(z == blocks - 1)
        def _():
            back_hop(q).start()

        return carry

    def whiten_last(q, carry):
        whiten(q, (1 - mirrored) * (bands - 1) * BAND, 1, lambda j: bands - 1)
        s = (bands - 1) * groups + q

        @pl.when(z == 0)
        def _():
            first_hop(s).start()

        @pl.when(z == blocks - 1)
        def _():
            back_hop(s).start()

        return carry

    def relay(s):
        next_hop(s).wait_recv()
        next_hop(s).start()

    def relay_early(s, count):
        @pl.when(z == 1)
        def _():
            for k in range(count):
                relay(s + k)

    lax.fori_loop(0, groups, whiten_inner, 0)
    relay_early(0, 1)

    @pl.when(z == 0)
    def _():
        @pl.loop(groups, (bands - 1) * groups)
        def _(s):
            first_hop(s).start()

    @pl.when(z == blocks - 1)
    def _():
        @pl.loop(groups, (bands - 1) * groups)
        def _(s):
            back_hop(s).start()

    @pl.when(takes_edge)
    def _():
        edge().wait_recv()

    lax.fori_loop(0, groups, whiten_last, 0)
    relay_early(1, 2)

    def transform(buffer, s):
        wide = jnp.concatenate([buffer[s, i] for i in range(GROUP)], axis=1)
        return jnp.dot(forward_ref[...], jnp.concatenate([wide, wide], axis=0), preferred_element_type=F32)

    tile = 32

    def power_into(total, s):
        for k in range(0, points, tile):
            gained = total[k : k + tile]
            for i in range(GROUP):
                lanes = slice(i * BAND, (i + 1) * BAND)
                real = spec[s, k : k + tile, lanes]
                imag = spec[s, points + k : points + k + tile, lanes]
                gained = gained + (real * real + imag * imag)
            total[k : k + tile] = gained

    def cross_into(total, near, far):
        for k in range(0, points, tile):
            gained_real = total[k : k + tile]
            gained_imag = total[points + k : points + k + tile]
            for i in range(GROUP):
                lanes = slice(i * BAND, (i + 1) * BAND)
                near_real = near[k : k + tile, lanes]
                near_imag = near[points + k : points + k + tile, lanes]
                far_real = far[k : k + tile, lanes]
                far_imag = far[points + k : points + k + tile, lanes]
                gained_real = gained_real + (near_real * far_real + near_imag * far_imag)
                gained_imag = gained_imag + (near_imag * far_real - near_real * far_imag)
            total[k : k + tile] = gained_real
            total[points + k : points + k + tile] = gained_imag

    def lags_of(values, columns):
        return jnp.dot(
            inverse_ref[:, :columns], values, preferred_element_type=F32, precision=lax.Precision.HIGHEST
        )

    def add_piece(c, first, piece):
        rows = pl.ds(first, points)
        stack[c, 0, rows] += piece[:points]
        stack[c, 1, rows] += piece[points:]

    def own_band(c, carry):
        sums[...] = jnp.zeros_like(sums)

        def step(q, inner):
            s = c * groups + q
            spec[s] = transform(white, s)
            power_into(sums, s)
            return inner

        lax.fori_loop(0, groups, step, 0)
        stack[c] = jnp.zeros(stack.shape[1:], F32)
        add_piece(c, 0, flag_ref[REACH + 1 : REACH + 2, :] * lags_of(sums[:points], points))
        relay_early(EARLY + c, 1)
        return carry

    lax.fori_loop(0, bands, own_band, 0)

    def counted_far(offset):
        return seen[offset : offset + 1, :] * seen[REACH + 1 + offset : REACH + 2 + offset, :]

    def counted_near(offset):
        return (1.0 - seen[offset : offset + 1, :]) * seen[REACH + 1 + offset : REACH + 2 + offset, :]

    @pl.when(z == 1)
    def _():
        flags_to(1).wait_recv()

        def band(c, carry):
            sums[...] = jnp.zeros_like(sums)

            def step(q, inner):
                s = c * groups + q

                @pl.when(s >= EARLY + bands)
                def _():
                    relay(s)

                other[...] = transform(far, s)
                cross_into(sums, other, spec.at[s])
                return inner

            lax.fori_loop(0, groups, step, 0)
            piece = lags_of(sums[...], 2 * points)
            near = (counted_near(1) * piece).astype(near_out.dtype)
            near_out[c, 0, :points] = near[:points]
            near_out[c, 1, :points] = near[points:]
            for target in range(2):
                to_first(c, 1, target, m, place(c)).start()
            add_piece(c, channels, counted_far(1) * piece)
            swap(c).start()
            return carry

        lax.fori_loop(0, bands, band, 0)

    @pl.when(z == 2)
    def _():
        flags_to(1).wait_recv()

        def band(c, carry):
            sums[...] = jnp.zeros_like(sums)
            sums_back[...] = jnp.zeros_like(sums_back)
            sums_far[...] = jnp.zeros_like(sums_far)

            def step(q, inner):
                s = c * groups + q
                back_hop(s).wait_recv()
                third[...] = transform(back, s)
                cross_into(sums_back, spec.at[s], third)
                next_hop(s).wait_recv()
                other[...] = transform(far, s)
                cross_into(sums, other, spec.at[s])
                cross_into(sums_far, other, third)
                return inner

            lax.fori_loop(0, groups, step, 0)
            piece = lags_of(sums[...], 2 * points)
            distant = lags_of(sums_far[...], 2 * points)
            near, beyond = counted_near(2) * piece, counted_near(3) * distant
            for part in range(2):
                top = part * points
                shared = near[top + channels : top + points] + beyond[top : top + channels]
                near_out[c, part, :channels] = near[top : top + channels].astype(near_out.dtype)
                near_out[c, part, channels:points] = shared.astype(near_out.dtype)
                near_out[c, part, points:] = beyond[top + channels : top + points].astype(near_out.dtype)
            for target in range(2):
                to_first(c, 2, target, m, place(c)).start()
            ahead = flag_ref[REACH + 2 : REACH + 3, :] * lags_of(sums_back[...], 2 * points)
            sent = flag_ref[1:2, :]
            piece_back[c, 0] = (sent * ahead).astype(piece_back.dtype)
            piece_back[c, 1] = (counted_far(3) * distant).astype(piece_back.dtype)
            to_next(c).start()
            add_piece(c, 2 * channels, counted_far(2) * piece)
            add_piece(c, channels, (1.0 - sent) * ahead)
            swap(c).start()
            return carry

        lax.fori_loop(0, bands, band, 0)

    @pl.when(z == blocks - 1)
    def _():
        def band(c, carry):
            to_next(c).wait_recv()
            add_piece(c, channels, arrived[c, 0].astype(F32))
            add_piece(c, 3 * channels, arrived[c, 1].astype(F32))
            swap(c).start()
            return carry

        lax.fori_loop(0, bands, band, 0)

    @pl.when(z == 0)
    def _():
        @pl.loop(0, bands)
        def _(c):
            swap(c).start()

    def collect(c, carry):
        mine = pl.ds(pl.multiple_of(m * half + place(c) * BAND, BAND), BAND)
        theirs = pl.ds(pl.multiple_of((1 - m) * half + place(c) * BAND, BAND), BAND)
        out_ref[:, :, mine] = stack[c, :, pl.ds(pl.multiple_of(m * kept, 8), kept)]
        swap(c).wait_recv()
        out_ref[:, :, theirs] = swapped[place(c)]
        swap(c).wait_send()
        return carry

    lax.fori_loop(0, bands, collect, 0)

    def add_near(target):
        def band(c, carry):
            for source in range(1, 3):
                _, low, high = near_rows(source, target)
                rows = slice(low - target * kept, high - target * kept)
                for sender in range(2):
                    to_first(c, source, target, sender, place(c)).wait_recv()
                    lanes = pl.ds(pl.multiple_of(sender * half + place(c) * BAND, BAND), BAND)
                    out_ref[:, rows, lanes] += near_in[source - 1, sender, place(c), :, rows].astype(F32)
            return carry

        lax.fori_loop(0, bands, band, 0)

    @pl.when((z == 0) & (m == 0))
    def _():
        add_near(0)

    @pl.when((z == 0) & (m == 1))
    def _():
        add_near(1)

    @pl.when(sends_edge)
    def _():
        edge().wait_send()

    @pl.when(z < 2)
    def _():
        @pl.loop(0, bands * groups)
        def _(s):
            next_hop(s).wait_send()

    @pl.when(z == blocks - 1)
    def _():
        @pl.loop(0, bands * groups)
        def _(s):
            back_hop(s).wait_send()

    @pl.when(z == 1)
    def _():
        @pl.loop(0, bands)
        def _(c):
            for target in range(2):
                to_first(c, 1, target, m, place(c)).wait_send()

    @pl.when(z == 2)
    def _():
        @pl.loop(0, bands)
        def _(c):
            for target in range(2):
                to_first(c, 2, target, m, place(c)).wait_send()
            to_next(c).wait_send()

    @pl.when(z == 0)
    def _():
        for block in range(1, blocks - 1):
            flags_to(block).wait_send()


def four_block_shards(spectra, counts, owners):
    parts, windows, channels, bins = spectra.shape
    halves, blocks = lax.axis_size("pairs"), lax.axis_size("cable")
    half, points = bins // halves, 2 * channels
    forward, inverse = channel_transforms(channels, 1.0 / math.sqrt(windows * channels))
    bands, groups = half // BAND, windows // GROUP
    pieces = bands * groups
    rows = (REACH + 2) * channels
    kept = rows // halves
    block = pltpu.VMEM((pieces, GROUP, points, BAND), jnp.bfloat16)
    spectrum = pltpu.VMEM((2 * points, GROUP * BAND), F32)
    sums = pltpu.VMEM((2 * points, BAND), F32)

    def lags(lead):
        return pltpu.VMEM(lead + (2 * points, BAND), jnp.bfloat16)

    dma = pltpu.SemaphoreType.DMA
    out = pl.pallas_call(
        stack_kernel,
        out_shape=jax.ShapeDtypeStruct((2, kept, bins), F32),
        in_specs=[
            pl.BlockSpec(memory_space=pl.ANY),
            pl.BlockSpec(memory_space=pltpu.SMEM),
            pl.BlockSpec(memory_space=pltpu.SMEM),
            pl.BlockSpec(memory_space=pltpu.VMEM),
            pl.BlockSpec(memory_space=pltpu.VMEM),
            pl.BlockSpec(memory_space=pltpu.VMEM),
        ],
        out_specs=pl.BlockSpec(memory_space=pltpu.VMEM),
        scratch_shapes=[
            pltpu.VMEM((2, windows, channels, half + 2 * EDGE), jnp.bfloat16),
            pltpu.VMEM((2 * (REACH + 1), BAND), F32),
            block, block, block,
            pltpu.VMEM((pieces, 2 * points, GROUP * BAND), F32),
            spectrum, spectrum, sums, sums, sums,
            pltpu.VMEM((bands, 2, rows, BAND), F32),
            pltpu.VMEM((bands, 2, points + channels, BAND), jnp.bfloat16),
            lags((bands, 2)),
            pltpu.VMEM((2, halves, bands, 2, kept, BAND), jnp.bfloat16),
            lags((bands, 2)),
            pltpu.VMEM((bands, 2, kept, BAND), F32),
            pltpu.VMEM((2 * (REACH + 1), BAND), F32),
            dma((pieces,)), dma((pieces,)), dma((pieces,)), dma((pieces,)),
            dma((halves, bands)), dma((2, halves, bands)),
            dma((bands,)), dma((bands,)), dma((bands,)), dma((bands,)),
            dma((blocks - 1,)), dma((1,)),
            dma((groups,)), dma((1,)), dma((1,)),
        ],
        compiler_params=pltpu.CompilerParams(
            collective_id=0, has_side_effects=True, vmem_limit_bytes=60 * 1024 * 1024
        ),
    )(spectra, counts, owners, smoothing_window(), forward, inverse)
    return out[:, None]


def solution(mesh):
    sizes = dict(mesh.shape)
    fits = sizes["cable"] == REACH + 1 and sizes["pairs"] == 2
    shards = four_block_shards if fits else general_shards
    placed = (
        P("groups", None, "cable", "bins"),
        P(("groups", "cable")),
        P(("groups", "cable"), None),
    )
    return jax.shard_map(
        shards,
        mesh=mesh,
        in_specs=placed,
        out_specs=P("groups", "cable", "pairs", "bins"),
        check_vma=False,
    )
```

```python
import math

import jax
import jax.numpy as jnp
import numpy as np
from jax import lax
from jax.experimental import pallas as pl
from jax.experimental.pallas import tpu as pltpu
from jax.sharding import PartitionSpec as P

REACH = 3
HALF_WIDTH = 32


epsilon = 1e-06
band_rows = 16


def with_halo(x, sides, width):
    for axis, dim in sides:
        count, length = (lax.axis_size(axis), x.shape[dim])
        up = [(i, (i + 1) % count) for i in range(count - 1)]
        down = [(j, i) for i, j in up]
        last = lax.slice_in_dim(x, length - width, length, axis=dim)
        first = lax.slice_in_dim(x, 0, width, axis=dim)
        before = lax.ppermute(last, axis, up)
        after = lax.ppermute(first, axis, down)
        x = jnp.concatenate([before, x, after], axis=dim)
    return x


def from_behind(block, axis, distance):
    devices = range(lax.axis_size(axis))
    route = [(i - distance, i) for i in devices if i - distance in devices]
    return lax.ppermute(block, axis, route)


def whiten_rows(spectra):
    real_part = spectra[0].astype(jnp.float32)
    imag_part = spectra[1].astype(jnp.float32)
    power_sum = real_part * real_part + imag_part * imag_part
    padded = with_halo(power_sum, (("bins", 2),), HALF_WIDTH)
    window_len = 2 * HALF_WIDTH + 1
    window_sum = lax.reduce_window(
        padded, jnp.zeros((), padded.dtype), lax.add, (1, 1, window_len), (1, 1, 1), "VALID"
    )
    inverse_amp = lax.rsqrt(window_sum / window_len + epsilon)
    return jnp.stack(
        [
            (real_part * inverse_amp).astype(jnp.bfloat16),
            (imag_part * inverse_amp).astype(jnp.bfloat16),
        ]
    )


def make_lag_table(col_count):
    flattened = jnp.arange(band_rows * col_count)
    row_of = flattened // col_count
    col_of = flattened % col_count
    lag_lanes = jnp.arange(col_count + band_rows - 1)
    return (lag_lanes[None, :] == (col_of - row_of + band_rows - 1)[:, None]).astype(jnp.bfloat16)


def lag_stack(pair_block, lag_table):
    freq_count, row_count, col_count = pair_block.shape
    group_count = row_count // band_rows
    grouped = pair_block.reshape(freq_count, group_count, band_rows * col_count)
    banded = jnp.einsum("fgk,ku->fgu", grouped, lag_table, preferred_element_type=jnp.float32)
    lag_sums = jnp.zeros((freq_count, col_count + row_count - 1), jnp.float32)
    for row_group in range(group_count):
        first_lag = row_count - band_rows * (row_group + 1)
        lag_sums = lag_sums.at[:, first_lag : first_lag + col_count + band_rows - 1].add(
            banded[:, row_group]
        )
    return lag_sums.T


def correlate(left_rows, right_rows, factor, lag_table):
    left_real = jnp.concatenate([left_rows[0], left_rows[1]], axis=0)
    left_imag = jnp.concatenate([left_rows[1], -left_rows[0]], axis=0)
    right_both = jnp.concatenate([right_rows[0], right_rows[1]], axis=0)
    corr_real = (
        jnp.einsum("wif,wjf->fij", left_real, right_both, preferred_element_type=jnp.float32)
        * factor
    ).astype(jnp.bfloat16)
    corr_imag = (
        jnp.einsum("wif,wjf->fij", left_imag, right_both, preferred_element_type=jnp.float32)
        * factor
    ).astype(jnp.bfloat16)
    return jnp.stack([lag_stack(corr_real, lag_table), lag_stack(corr_imag, lag_table)])


def general_shards(spectra, counts, owners):
    pair_devs = lax.axis_size("pairs")
    member = lax.axis_index("pairs")
    channels = spectra.shape[2]
    half_rows = channels // pair_devs
    source = whiten_rows(spectra)
    receiver = lax.dynamic_slice_in_dim(source, member * half_rows, half_rows, 2)
    block_count = lax.axis_size("cable")
    cable_index = lax.axis_index("cable")
    live_count = jnp.minimum(counts[0], block_count - cable_index)
    panels = {0: receiver}
    for offset in range(1, REACH + 1):
        panels[offset] = from_behind(receiver, "cable", -offset)
    factor = 1.0 / math.sqrt(source.shape[1] * channels)
    lag_table = make_lag_table(half_rows)
    freq_count = source.shape[3]
    stacks = jnp.zeros((2, (REACH + 2) * channels, freq_count), jnp.float32)
    for offset in range(REACH + 1):
        lag_piece = correlate(source, panels[offset], factor, lag_table)
        weight = (offset < live_count).astype(jnp.float32)
        if offset == 0:
            kept_here = weight * lag_piece
        else:
            sent_away = owners[0, offset].astype(jnp.float32)
            arrived = from_behind(weight * sent_away * lag_piece, "cable", offset)
            kept_here = weight * (1.0 - sent_away) * lag_piece + arrived
        first_lag = offset * channels + member * half_rows
        current = lax.dynamic_slice_in_dim(stacks, first_lag, kept_here.shape[1], 1)
        stacks = lax.dynamic_update_slice_in_dim(stacks, current + kept_here, first_lag, 1)
    summed = lax.psum_scatter(stacks, "pairs", scatter_dimension=1, tiled=True)
    return summed[:, None]


EDGE = 128
BAND = 128
GROUP = 2
EARLY = 3
F32 = jnp.float32
MESH = pl.DeviceIdType.MESH


def channel_transforms(channels, factor):
    points = 2 * channels
    index = np.arange(points)
    angle = 2 * np.pi * np.outer(index, np.arange(channels)) / points
    cos, sin = np.cos(angle), np.sin(angle)
    full = np.block([[cos, sin], [-sin, cos]])
    high = full.astype(jnp.bfloat16)
    low = (full - high.astype(np.float64)).astype(jnp.bfloat16)
    forward = np.concatenate([high, low], axis=1)
    angle = 2 * np.pi * np.outer(index - (channels - 1), index) / points
    cos, sin = np.cos(angle), np.sin(angle)
    cos[-1], sin[-1] = 0.0, 0.0
    inverse = np.block([[cos, sin], [-sin, cos]]) * (factor / points)
    return jnp.asarray(forward), jnp.asarray(inverse.astype(np.float32))


def smoothing_window():
    distance = np.arange(BAND + 2 * EDGE)[:, None] - (np.arange(BAND)[None, :] + EDGE)
    ones = (np.abs(distance) <= HALF_WIDTH).astype(jnp.bfloat16)
    return jnp.asarray(np.concatenate([ones, ones], axis=0))


def stack_kernel(
    spectra_ref, counts_ref, owners_ref, window_ref, forward_ref, inverse_ref, out_ref,
    x_ref, flag_ref, white, far, back, spec, other, third, sums, sums_back, sums_far, stack, near_out, piece_back, near_in, arrived, swapped, seen,
    chain_send, chain_recv, back_send, back_recv, piece_send, piece_recv,
    next_send, next_recv, swap_send, swap_recv, flag_send, flag_recv, load_sem, edge_send, edge_recv,
):
    windows, channels = x_ref.shape[1:3]
    half = x_ref.shape[3] - 2 * EDGE
    bands, groups = half // BAND, windows // GROUP
    points = 2 * channels
    kept = out_ref.shape[1]
    blocks, halves = lax.axis_size("cable"), lax.axis_size("pairs")
    z, m = lax.axis_index("cable"), lax.axis_index("pairs")
    cuts, x = lax.axis_size("bins"), lax.axis_index("bins")
    bins = spectra_ref.shape[3]
    first = m == 0
    mirrored = jnp.where((x > 0) & (first | (x == cuts - 1)), 1, 0)
    onward = {"cable": lax.rem(z + 1, blocks)}
    backward = {"cable": lax.rem(z + blocks - 1, blocks)}
    partner = {"pairs": lax.rem(m + 1, halves)}

    def remote(source, target, send, recv, device):
        return pltpu.make_async_remote_copy(
            src_ref=source, dst_ref=target, send_sem=send, recv_sem=recv, device_id=device, device_id_type=MESH
        )

    def first_hop(s):
        return remote(white.at[s], far.at[s], chain_send.at[s], chain_recv.at[s], onward)

    def next_hop(s):
        return remote(far.at[s], far.at[s], chain_send.at[s], chain_recv.at[s], onward)

    def back_hop(s):
        return remote(white.at[s], back.at[s], back_send.at[s], back_recv.at[s], backward)

    def near_rows(source, target):
        begin, end = source * channels, source * channels + points + (source - 1) * channels
        return begin, max(begin, target * kept), min(end, (target + 1) * kept)

    def to_first(c, source, target, sender, spot_of):
        begin, low, high = near_rows(source, target)
        return remote(
            near_out.at[c, :, low - begin : high - begin],
            near_in.at[source - 1, sender, spot_of, :, low - target * kept : high - target * kept],
            piece_send.at[target, c],
            piece_recv.at[source - 1, sender, spot_of],
            {"cable": 0, "pairs": target},
        )

    def to_next(c):
        return remote(piece_back.at[c], arrived.at[c], next_send.at[c], next_recv.at[c], onward)

    def swap(c):
        rows = pl.ds(pl.multiple_of((1 - m) * kept, 8), kept)
        return remote(
            stack.at[c, :, rows], swapped.at[place(c)], swap_send.at[c], swap_recv.at[place(c)], partner
        )

    def place(c):
        return c + mirrored * (bands - 1 - 2 * c)

    def load(q):
        near = pl.multiple_of(m * (half - EDGE), EDGE)
        spot = pl.multiple_of((1 - m) * EDGE, EDGE)
        rows = pl.ds(q * GROUP, GROUP)
        return pltpu.make_async_copy(
            spectra_ref.at[:, rows, :, pl.ds(near, half + EDGE)],
            x_ref.at[:, rows, :, pl.ds(spot, half + EDGE)],
            load_sem.at[q],
        )

    spot = pl.ds(pl.multiple_of(m * (half + EDGE), EDGE), EDGE)

    def edge():
        source = pl.ds(pl.multiple_of((1 - m) * (bins - EDGE), EDGE), EDGE)
        target = {"bins": lax.rem(x + cuts + 1 - 2 * m, cuts)}
        return remote(
            spectra_ref.at[:, :, :, source], x_ref.at[:, :, :, spot], edge_send.at[0], edge_recv.at[0], target
        )

    def flags_to(block):
        return remote(flag_ref, seen, flag_send.at[block - 1], flag_recv.at[0], {"cable": block})

    for q in range(groups):
        load(q).start()
    live = jnp.minimum(counts_ref[0], blocks - z)
    for offset in range(REACH + 1):
        flag_ref[offset : offset + 1, :] = jnp.full((1, BAND), owners_ref[0, offset].astype(F32))
        weight = jnp.where(offset < live, 1.0, 0.0)
        flag_ref[REACH + 1 + offset : REACH + 2 + offset, :] = jnp.full((1, BAND), weight)
    barrier = pltpu.get_barrier_semaphore()
    for step in range(1, blocks):
        pl.semaphore_signal(barrier, inc=1, device_id={"cable": lax.rem(z + step, blocks)}, device_id_type=MESH)
        across = {"cable": lax.rem(z + step, blocks), "pairs": lax.rem(m + 1, halves)}
        pl.semaphore_signal(barrier, inc=1, device_id=across, device_id_type=MESH)
    pl.semaphore_signal(barrier, inc=1, device_id=partner, device_id_type=MESH)
    for step in range(1, cuts):
        pl.semaphore_signal(barrier, inc=1, device_id={"bins": lax.rem(x + step, cuts)}, device_id_type=MESH)
    pl.semaphore_wait(barrier, 2 * blocks + cuts - 2)
    sends_edge = (first & (x < cuts - 1)) | (~first & (x > 0))
    takes_edge = (first & (x > 0)) | (~first & (x < cuts - 1))

    @pl.when(sends_edge)
    def _():
        edge().start()

    @pl.when(~takes_edge)
    def _():
        x_ref[:, :, :, spot] = jnp.zeros((2, windows, channels, EDGE), x_ref.dtype)


    @pl.when(z == 0)
    def _():
        for block in range(1, blocks - 1):
            flags_to(block).start()

    def whiten(q, begin, count, store):
        lanes = pl.ds(pl.multiple_of(begin, BAND), count * BAND + 2 * EDGE)
        reals, imags, highs, lows = [], [], [], []
        for i in range(GROUP):
            real = x_ref[0, q * GROUP + i, :, lanes].astype(F32)
            imag = x_ref[1, q * GROUP + i, :, lanes].astype(F32)
            power = real * real + imag * imag
            high = power.astype(jnp.bfloat16)
            reals.append(real)
            imags.append(imag)
            highs.append(high)
            lows.append((power - high.astype(F32)).astype(jnp.bfloat16))
        high = jnp.concatenate(highs, axis=0)
        low = jnp.concatenate(lows, axis=0)
        for j in range(count):
            reach = slice(j * BAND, (j + 1) * BAND + 2 * EDGE)
            terms = jnp.concatenate([high[:, reach], low[:, reach]], axis=1)
            total = jnp.dot(terms, window_ref[...], preferred_element_type=F32)
            gain = lax.rsqrt(total / (2 * HALF_WIDTH + 1) + epsilon)
            here = slice(EDGE + j * BAND, EDGE + (j + 1) * BAND)
            slot = store(j) * groups + q
            for i in range(GROUP):
                rows = gain[i * channels : (i + 1) * channels]
                white[slot, i, :channels] = (reals[i][:, here] * rows).astype(jnp.bfloat16)
                white[slot, i, channels:] = (imags[i][:, here] * rows).astype(jnp.bfloat16)

    def whiten_inner(q, carry):
        load(q).wait()
        whiten(q, mirrored * BAND, bands - 1, lambda j: j + mirrored * (bands - 2 - 2 * j))

        @pl.when(z == 0)
        def _():
            first_hop(q).start()

        @pl.when(z == blocks - 1)
        def _():
            back_hop(q).start()

        return carry

    def whiten_last(q, carry):
        whiten(q, (1 - mirrored) * (bands - 1) * BAND, 1, lambda j: bands - 1)
        s = (bands - 1) * groups + q

        @pl.when(z == 0)
        def _():
            first_hop(s).start()

        @pl.when(z == blocks - 1)
        def _():
            back_hop(s).start()

        return carry

    def relay(s):
        next_hop(s).wait_recv()
        next_hop(s).start()

    def relay_early(s, count):
        @pl.when(z == 1)
        def _():
            for k in range(count):
                relay(s + k)

    lax.fori_loop(0, groups, whiten_inner, 0)
    relay_early(0, 1)

    @pl.when(z == 0)
    def _():
        @pl.loop(groups, (bands - 1) * groups)
        def _(s):
            first_hop(s).start()

    @pl.when(z == blocks - 1)
    def _():
        @pl.loop(groups, (bands - 1) * groups)
        def _(s):
            back_hop(s).start()

    @pl.when(takes_edge)
    def _():
        edge().wait_recv()

    lax.fori_loop(0, groups, whiten_last, 0)
    relay_early(1, 2)

    def transform(buffer, s):
        wide = jnp.concatenate([buffer[s, i] for i in range(GROUP)], axis=1)
        return jnp.dot(forward_ref[...], jnp.concatenate([wide, wide], axis=0), preferred_element_type=F32)

    tile = 32

    def power_into(total, s):
        for k in range(0, points, tile):
            gained = total[k : k + tile]
            for i in range(GROUP):
                lanes = slice(i * BAND, (i + 1) * BAND)
                real = spec[s, k : k + tile, lanes]
                imag = spec[s, points + k : points + k + tile, lanes]
                gained = gained + (real * real + imag * imag)
            total[k : k + tile] = gained

    def cross_into(total, near, far):
        for k in range(0, points, tile):
            gained_real = total[k : k + tile]
            gained_imag = total[points + k : points + k + tile]
            for i in range(GROUP):
                lanes = slice(i * BAND, (i + 1) * BAND)
                near_real = near[k : k + tile, lanes]
                near_imag = near[points + k : points + k + tile, lanes]
                far_real = far[k : k + tile, lanes]
                far_imag = far[points + k : points + k + tile, lanes]
                gained_real = gained_real + (near_real * far_real + near_imag * far_imag)
                gained_imag = gained_imag + (near_imag * far_real - near_real * far_imag)
            total[k : k + tile] = gained_real
            total[points + k : points + k + tile] = gained_imag

    def lags_of(values, columns):
        return jnp.dot(
            inverse_ref[:, :columns], values, preferred_element_type=F32, precision=lax.Precision.HIGHEST
        )

    def add_piece(c, first, piece):
        rows = pl.ds(first, points)
        stack[c, 0, rows] += piece[:points]
        stack[c, 1, rows] += piece[points:]

    def own_band(c, carry):
        sums[...] = jnp.zeros_like(sums)

        def step(q, inner):
            s = c * groups + q
            spec[s] = transform(white, s)
            power_into(sums, s)
            return inner

        lax.fori_loop(0, groups, step, 0)
        stack[c] = jnp.zeros(stack.shape[1:], F32)
        add_piece(c, 0, flag_ref[REACH + 1 : REACH + 2, :] * lags_of(sums[:points], points))
        relay_early(EARLY + c, 1)
        return carry

    lax.fori_loop(0, bands, own_band, 0)

    def counted_far(offset):
        return seen[offset : offset + 1, :] * seen[REACH + 1 + offset : REACH + 2 + offset, :]

    def counted_near(offset):
        return (1.0 - seen[offset : offset + 1, :]) * seen[REACH + 1 + offset : REACH + 2 + offset, :]

    @pl.when(z == 1)
    def _():
        flags_to(1).wait_recv()

        def band(c, carry):
            sums[...] = jnp.zeros_like(sums)

            def step(q, inner):
                s = c * groups + q

                @pl.when(s >= EARLY + bands)
                def _():
                    relay(s)

                other[...] = transform(far, s)
                cross_into(sums, other, spec.at[s])
                return inner

            lax.fori_loop(0, groups, step, 0)
            piece = lags_of(sums[...], 2 * points)
            near = (counted_near(1) * piece).astype(near_out.dtype)
            near_out[c, 0, :points] = near[:points]
            near_out[c, 1, :points] = near[points:]
            for target in range(2):
                to_first(c, 1, target, m, place(c)).start()
            add_piece(c, channels, counted_far(1) * piece)
            swap(c).start()
            return carry

        lax.fori_loop(0, bands, band, 0)

    @pl.when(z == 2)
    def _():
        flags_to(1).wait_recv()

        def band(c, carry):
            sums[...] = jnp.zeros_like(sums)
            sums_back[...] = jnp.zeros_like(sums_back)
            sums_far[...] = jnp.zeros_like(sums_far)

            def step(q, inner):
                s = c * groups + q
                back_hop(s).wait_recv()
                third[...] = transform(back, s)
                cross_into(sums_back, spec.at[s], third)

                @pl.when(q == groups - 1)
                def _():
                    sums_back[...] = flag_ref[REACH + 2 : REACH + 3, :] * lags_of(sums_back[...], 2 * points)

                next_hop(s).wait_recv()
                other[...] = transform(far, s)
                cross_into(sums, other, spec.at[s])
                cross_into(sums_far, other, third)
                return inner

            lax.fori_loop(0, groups, step, 0)
            both = lags_of(jnp.concatenate([sums[...], sums_far[...]], axis=1), 2 * points)
            piece, distant = both[:, :BAND], both[:, BAND:]
            near, beyond = counted_near(2) * piece, counted_near(3) * distant
            for part in range(2):
                top = part * points
                shared = near[top + channels : top + points] + beyond[top : top + channels]
                near_out[c, part, :channels] = near[top : top + channels].astype(near_out.dtype)
                near_out[c, part, channels:points] = shared.astype(near_out.dtype)
                near_out[c, part, points:] = beyond[top + channels : top + points].astype(near_out.dtype)
            for target in range(2):
                to_first(c, 2, target, m, place(c)).start()
            ahead = sums_back[...]
            sent = flag_ref[1:2, :]
            piece_back[c, 0] = (sent * ahead).astype(piece_back.dtype)
            piece_back[c, 1] = (counted_far(3) * distant).astype(piece_back.dtype)
            to_next(c).start()
            add_piece(c, 2 * channels, counted_far(2) * piece)
            add_piece(c, channels, (1.0 - sent) * ahead)
            swap(c).start()
            return carry

        lax.fori_loop(0, bands, band, 0)

    @pl.when(z == blocks - 1)
    def _():
        def band(c, carry):
            to_next(c).wait_recv()
            add_piece(c, channels, arrived[c, 0].astype(F32))
            add_piece(c, 3 * channels, arrived[c, 1].astype(F32))
            swap(c).start()
            return carry

        lax.fori_loop(0, bands, band, 0)

    @pl.when(z == 0)
    def _():
        @pl.loop(0, bands)
        def _(c):
            swap(c).start()

    def collect(c, carry):
        mine = pl.ds(pl.multiple_of(m * half + place(c) * BAND, BAND), BAND)
        theirs = pl.ds(pl.multiple_of((1 - m) * half + place(c) * BAND, BAND), BAND)
        out_ref[:, :, mine] = stack[c, :, pl.ds(pl.multiple_of(m * kept, 8), kept)]
        swap(c).wait_recv()
        out_ref[:, :, theirs] = swapped[place(c)]
        swap(c).wait_send()
        return carry

    lax.fori_loop(0, bands, collect, 0)

    def add_near(target):
        def band(c, carry):
            for source in range(1, 3):
                _, low, high = near_rows(source, target)
                rows = slice(low - target * kept, high - target * kept)
                for sender in range(2):
                    to_first(c, source, target, sender, place(c)).wait_recv()
                    lanes = pl.ds(pl.multiple_of(sender * half + place(c) * BAND, BAND), BAND)
                    out_ref[:, rows, lanes] += near_in[source - 1, sender, place(c), :, rows].astype(F32)
            return carry

        lax.fori_loop(0, bands, band, 0)

    @pl.when((z == 0) & (m == 0))
    def _():
        add_near(0)

    @pl.when((z == 0) & (m == 1))
    def _():
        add_near(1)

    @pl.when(sends_edge)
    def _():
        edge().wait_send()

    @pl.when(z < 2)
    def _():
        @pl.loop(0, bands * groups)
        def _(s):
            next_hop(s).wait_send()

    @pl.when(z == blocks - 1)
    def _():
        @pl.loop(0, bands * groups)
        def _(s):
            back_hop(s).wait_send()

    @pl.when(z == 1)
    def _():
        @pl.loop(0, bands)
        def _(c):
            for target in range(2):
                to_first(c, 1, target, m, place(c)).wait_send()

    @pl.when(z == 2)
    def _():
        @pl.loop(0, bands)
        def _(c):
            for target in range(2):
                to_first(c, 2, target, m, place(c)).wait_send()
            to_next(c).wait_send()

    @pl.when(z == 0)
    def _():
        for block in range(1, blocks - 1):
            flags_to(block).wait_send()


def four_block_shards(spectra, counts, owners):
    parts, windows, channels, bins = spectra.shape
    halves, blocks = lax.axis_size("pairs"), lax.axis_size("cable")
    half, points = bins // halves, 2 * channels
    forward, inverse = channel_transforms(channels, 1.0 / math.sqrt(windows * channels))
    bands, groups = half // BAND, windows // GROUP
    pieces = bands * groups
    rows = (REACH + 2) * channels
    kept = rows // halves
    block = pltpu.VMEM((pieces, GROUP, points, BAND), jnp.bfloat16)
    spectrum = pltpu.VMEM((2 * points, GROUP * BAND), F32)
    sums = pltpu.VMEM((2 * points, BAND), F32)

    def lags(lead):
        return pltpu.VMEM(lead + (2 * points, BAND), jnp.bfloat16)

    dma = pltpu.SemaphoreType.DMA
    out = pl.pallas_call(
        stack_kernel,
        out_shape=jax.ShapeDtypeStruct((2, kept, bins), F32),
        in_specs=[
            pl.BlockSpec(memory_space=pl.ANY),
            pl.BlockSpec(memory_space=pltpu.SMEM),
            pl.BlockSpec(memory_space=pltpu.SMEM),
            pl.BlockSpec(memory_space=pltpu.VMEM),
            pl.BlockSpec(memory_space=pltpu.VMEM),
            pl.BlockSpec(memory_space=pltpu.VMEM),
        ],
        out_specs=pl.BlockSpec(memory_space=pltpu.VMEM),
        scratch_shapes=[
            pltpu.VMEM((2, windows, channels, half + 2 * EDGE), jnp.bfloat16),
            pltpu.VMEM((2 * (REACH + 1), BAND), F32),
            block, block, block,
            pltpu.VMEM((pieces, 2 * points, GROUP * BAND), F32),
            spectrum, spectrum, sums, sums, sums,
            pltpu.VMEM((bands, 2, rows, BAND), F32),
            pltpu.VMEM((bands, 2, points + channels, BAND), jnp.bfloat16),
            lags((bands, 2)),
            pltpu.VMEM((2, halves, bands, 2, kept, BAND), jnp.bfloat16),
            lags((bands, 2)),
            pltpu.VMEM((bands, 2, kept, BAND), F32),
            pltpu.VMEM((2 * (REACH + 1), BAND), F32),
            dma((pieces,)), dma((pieces,)), dma((pieces,)), dma((pieces,)),
            dma((halves, bands)), dma((2, halves, bands)),
            dma((bands,)), dma((bands,)), dma((bands,)), dma((bands,)),
            dma((blocks - 1,)), dma((1,)),
            dma((groups,)), dma((1,)), dma((1,)),
        ],
        compiler_params=pltpu.CompilerParams(
            collective_id=0, has_side_effects=True, vmem_limit_bytes=60 * 1024 * 1024
        ),
    )(spectra, counts, owners, smoothing_window(), forward, inverse)
    return out[:, None]


def solution(mesh):
    sizes = dict(mesh.shape)
    fits = sizes["cable"] == REACH + 1 and sizes["pairs"] == 2
    shards = four_block_shards if fits else general_shards
    placed = (
        P("groups", None, "cable", "bins"),
        P(("groups", "cable")),
        P(("groups", "cable"), None),
    )
    return jax.shard_map(
        shards,
        mesh=mesh,
        in_specs=placed,
        out_specs=P("groups", "cable", "pairs", "bins"),
        check_vma=False,
    )
```
